256 devices in a mesh: group: 8 (over y, core), inner: 32 (over x, z).
Axes of the slice: x: 4, y: 4, z: 8, core: 2. Of those that a mesh axis runs over, the one named last changes fastest.
Arguments:
- left_part: bfloat16 [262144, 256], P(('group', 'inner')), may hold values from -12 to 12
- right_part: bfloat16 [262144, 256], P(('group', 'inner')), may hold values from -12 to 12
- relation: bfloat16 [256, 256], replicated, may hold values from -0.19 to 1.19
- src_index: int32 [256, 4, 512], P(('group', 'inner')), may hold values from 0 to 1023
- dst_index: int32 [256, 4, 512], P(('group', 'inner')), may hold values from 0 to 1023
- lengths: int32 [256, 4], P(('group', 'inner')), may hold values from 1 to 512, 1280 in all within a row
Outputs:
- left_out: bfloat16 [262144, 256], P(('group', 'inner'))
- right_out: bfloat16 [262144, 256], P(('group', 'inner'))
- relation_out: float32 [256, 256], replicated
The draws below stay inside these ranges and needn't reach their ends.
All inputs are finite; a program needn't handle non-finite values.
Results may differ from the reference program's by a relative error of at most 0.012.
The reference program's roundings to bfloat16 on the way (of `holding`, `picked`, `queries`, `coeffs` and `query_grad`) count: a program that leaves them out, or rounds other values in their place, can miss the bound.
Values may be sent and summed in bfloat16 or wider, within the bound.
No kernel may reach another device: no remote copies, remote signals or barrier semaphores. Data moves between devices by JAX's collectives and lax.ppermute only.
A program may use at most 64 MiB of HBM per device.

```python
import math
import jax
import jax.numpy as jnp
import numpy as np
from jax import lax

D = 256
P_SIZE = 1024
E = 512
MEETINGS = 4
PARTS_SIZE = 256
N_GROUP = 8
N_INNER = 32


def embed_base(key, salt):
    normal_draw = jnp.clip(jax.random.normal(jax.random.fold_in(key, salt), (PARTS_SIZE * P_SIZE, D), jnp.float32), -6.0, 6.0)
    return normal_draw


def draw_left_part(key, part):
    values = embed_base(key, 1)
    return jnp.clip(values, -12.0, 12.0).astype(jnp.bfloat16)


def draw_right_part(key, part):
    values = embed_base(key, 2)
    return jnp.clip(values, -12.0, 12.0).astype(jnp.bfloat16)


def draw_relation(key, part):
    normal_draw = jnp.clip(jax.random.normal(jax.random.fold_in(key, 3), (D, D), jnp.float32), -6.0, 6.0) * (0.5 * D ** (-0.5))
    positions = jnp.arange(D)
    identity = (positions[:, None] == positions[None, :]).astype(jnp.float32)
    return (identity + normal_draw).astype(jnp.bfloat16)


def place_ends(drawn, own_key, least, high):
    longest = drawn.shape.index(max(drawn.shape))
    spots = []
    for shift in (0, 1):
        where = [jax.random.randint(jax.random.fold_in(own_key, axis), (), 0, length) for axis, length in enumerate(drawn.shape)]
        where[longest] = (where[longest] + shift) % drawn.shape[longest]
        spots.append(tuple(where))
    return drawn.at[spots[0]].set(least).at[spots[1]].set(high)


def length_profile(number_of, total, limit, slope):
    weights = [(1 << 20) // math.isqrt(rank ** slope) + 1 for rank in range(2, number_of + 1)]
    spare, counts = total - limit - (number_of - 1), [1] * (number_of - 1)
    while spare > 0:
        candidates = [i for i in range(number_of - 1) if counts[i] < limit]
        mass, budget = sum([weights[i] for i in candidates]), spare
        for i in candidates:
            more = min(limit - counts[i], max(1, budget * weights[i] // mass), spare)
            counts[i] = counts[i] + more
            spare = spare - more
    return np.array([limit] + counts)


def uneven_parts(key, number_of, total, reach, skew):
    if number_of == 2:
        one = jax.random.randint(key, (), max(1, total - reach), min(reach, total - 1) + 1)
        return jnp.stack([one, total - one])
    tallies = jnp.asarray(length_profile(number_of, total, reach, skew), jnp.int32)
    pairs = (number_of - 1) // 2
    donor, sink = tallies[1:1 + 2 * pairs:2], tallies[2:2 + 2 * pairs:2]
    slack = jnp.minimum(donor - 1, reach - sink)
    passed = jax.random.randint(jax.random.fold_in(key, 1), (pairs,), 0, 1 << 20) % (slack + 1)
    tallies = tallies.at[1:1 + 2 * pairs:2].set(donor - passed).at[2:2 + 2 * pairs:2].set(sink + passed)
    return tallies[jax.random.permutation(jax.random.fold_in(key, 2), number_of)]


def setup_inputs(seed: int = 0) -> dict:
    key_of = jax.random.split(jax.random.key(seed), 7)
    return {
        "left_part": draw_left_part(jax.random.fold_in(key_of[6], 71), 0),
        "right_part": draw_right_part(jax.random.fold_in(key_of[6], 71), 0),
        "relation": draw_relation(jax.random.fold_in(key_of[6], 71), 0),
        "src_index": place_ends(jax.random.randint(key_of[3], (PARTS_SIZE, MEETINGS, E), 0, P_SIZE), jax.random.fold_in(key_of[3], 1), 0, P_SIZE - 1).astype(jnp.int32),
        "dst_index": place_ends(jax.random.randint(key_of[4], (PARTS_SIZE, MEETINGS, E), 0, P_SIZE), jax.random.fold_in(key_of[4], 1), 0, P_SIZE - 1).astype(jnp.int32),
        "lengths": jax.vmap(lambda own: uneven_parts(own, MEETINGS, 5 * E // 2, E, 2))(jax.random.split(key_of[5], PARTS_SIZE)).reshape((PARTS_SIZE, MEETINGS)).astype(jnp.int32),
    }


SCORE_SCALE = 0.1875
LR_EMBED = 0.5
LR_RELATION = 0.02


def bucket(left_block, holding, relation, src_row, dst_row, length):
    picked = jnp.take(left_block, src_row, axis=0)
    queries = jnp.dot(picked, relation, preferred_element_type=jnp.float32).astype(jnp.bfloat16)
    scores = lax.dot_general(queries, holding, (((1,), (1,)), ((), ())), preferred_element_type=jnp.float32) * SCORE_SCALE
    maxima = jnp.max(scores, axis=1, keepdims=True)
    expos = jnp.exp(scores - maxima)
    softmax_w = expos / jnp.sum(expos, axis=1, keepdims=True)
    slot_ids = jnp.arange(src_row.shape[0], dtype=jnp.int32)
    live_mask = (slot_ids < length).astype(jnp.float32)
    columns = jnp.arange(holding.shape[0], dtype=jnp.int32)
    target = (columns[None, :] == dst_row[:, None]).astype(jnp.float32)
    coeffs = ((softmax_w - target) * live_mask[:, None]).astype(jnp.bfloat16)
    held_grad = lax.dot_general(coeffs, queries, (((0,), (0,)), ((), ())), preferred_element_type=jnp.float32) * SCORE_SCALE
    query_grad = (jnp.dot(coeffs, holding, preferred_element_type=jnp.float32) * SCORE_SCALE).astype(jnp.bfloat16)
    relation_grad = lax.dot_general(picked, query_grad, (((0,), (0,)), ((), ())), preferred_element_type=jnp.float32)
    row_grad = lax.dot_general(query_grad, relation, (((1,), (1,)), ((), ())), preferred_element_type=jnp.float32)
    left_grad = jax.ops.segment_sum(row_grad, src_row, num_segments=left_block.shape[0])
    new_left = (left_block.astype(jnp.float32) - LR_EMBED * left_grad).astype(jnp.bfloat16)
    new_holding = (holding.astype(jnp.float32) - LR_EMBED * held_grad).astype(jnp.bfloat16)
    return new_left, new_holding, relation_grad


def reference(left_part, right_part, relation, src_index, dst_index, lengths):
    part_count = N_GROUP * N_INNER
    log_inner = N_INNER.bit_length() - 1
    left_blocks = left_part.reshape(part_count, P_SIZE, D)
    holding = right_part.reshape(part_count, P_SIZE, D)
    part_ids = jnp.arange(part_count, dtype=jnp.int32)
    grad_total = jnp.zeros((D, D), jnp.float32)
    for meeting in range(MEETINGS):
        partner_ids = jnp.bitwise_xor(part_ids, jnp.int32(1 << (meeting % log_inner)))
        holding = jnp.take(holding, partner_ids, axis=0)

        def one_bucket(items):
            return bucket(items[0], items[1], relation, items[2], items[3], items[4])

        left_blocks, holding, grads = lax.map(one_bucket, (left_blocks, holding, src_index[:, meeting], dst_index[:, meeting], lengths[:, meeting]))
        grad_total = grad_total + jnp.sum(grads, axis=0)
    relation_out = relation.astype(jnp.float32) - LR_RELATION * grad_total
    return left_blocks.reshape(part_count * P_SIZE, D), holding.reshape(part_count * P_SIZE, D), relation_out
```

```python
import jax
import jax.numpy as jnp
from jax import lax
from jax.sharding import PartitionSpec as P

MEETINGS = 4


SCORE_SCALE = 0.1875
LR_EMBED = 0.5
LR_RELATION = 0.02


def swapped(value, axis, distance):
    mask = 2**distance
    pairs = [(source, source ^ mask) for source in range(lax.axis_size(axis))]
    return lax.ppermute(value, axis, pairs)


def summed_over_all(partial):
    axes = ("group", "inner")
    rows, width = partial.shape
    pieces = partial.astype(jnp.bfloat16).reshape(rows, 1, width)
    pieces = lax.all_to_all(pieces, axes, 0, 0)
    own_row = jnp.sum(pieces.astype(jnp.float32), axis=0).astype(jnp.bfloat16)
    copies = jnp.broadcast_to(own_row[None], (rows, 1, width))
    gathered = lax.all_to_all(copies, axes, 0, 0)
    return gathered.reshape(rows, width).astype(jnp.float32)


def bucket(left_block, holding, relation, src_row, dst_row, length):
    row_ids = jnp.arange(left_block.shape[0], dtype=jnp.int32)
    src_table = (src_row[:, None] == row_ids[None, :]).astype(jnp.bfloat16)
    picked = jnp.dot(src_table, left_block, preferred_element_type=jnp.float32).astype(jnp.bfloat16)
    queries = jnp.dot(picked, relation, preferred_element_type=jnp.float32).astype(jnp.bfloat16)
    scores = (
        lax.dot_general(
            queries, holding, (((1,), (1,)), ((), ())), preferred_element_type=jnp.float32
        )
        * SCORE_SCALE
    )
    maxima = jnp.max(scores, axis=1, keepdims=True)
    expos = jnp.exp(scores - maxima)
    softmax_w = expos / jnp.sum(expos, axis=1, keepdims=True)
    slot_ids = jnp.arange(src_row.shape[0], dtype=jnp.int32)
    live_mask = (slot_ids < length).astype(jnp.float32)
    columns = jnp.arange(holding.shape[0], dtype=jnp.int32)
    target = (columns[None, :] == dst_row[:, None]).astype(jnp.float32)
    coeffs = ((softmax_w - target) * live_mask[:, None]).astype(jnp.bfloat16)
    held_grad = (
        lax.dot_general(
            coeffs, queries, (((0,), (0,)), ((), ())), preferred_element_type=jnp.float32
        )
        * SCORE_SCALE
    )
    new_holding = (holding.astype(jnp.float32) - LR_EMBED * held_grad).astype(jnp.bfloat16)
    query_grad = (
        jnp.dot(coeffs, holding, preferred_element_type=jnp.float32) * SCORE_SCALE
    ).astype(jnp.bfloat16)
    relation_grad = lax.dot_general(
        picked, query_grad, (((0,), (0,)), ((), ())), preferred_element_type=jnp.float32
    )
    summed_rows = lax.dot_general(
        src_table, query_grad, (((0,), (0,)), ((), ())), preferred_element_type=jnp.float32
    )
    left_grad = lax.dot_general(
        summed_rows,
        relation.astype(jnp.float32),
        (((1,), (1,)), ((), ())),
        precision=lax.Precision.HIGHEST,
        preferred_element_type=jnp.float32,
    )
    new_left = (left_block.astype(jnp.float32) - LR_EMBED * left_grad).astype(jnp.bfloat16)
    return (new_left, new_holding, relation_grad)


def shards(left_part, right_part, relation, src_index, dst_index, lengths):
    log_inner = lax.axis_size("inner").bit_length() - 1
    left_block = left_part
    holding = right_part
    grad_total = jnp.zeros(relation.shape, jnp.float32)
    for meeting in range(MEETINGS):
        holding = swapped(holding, "inner", meeting % log_inner)
        left_block, holding, relation_grad = bucket(
            left_block,
            holding,
            relation,
            src_index[0, meeting],
            dst_index[0, meeting],
            lengths[0, meeting],
        )
        grad_total = grad_total + relation_grad
    grad_total = summed_over_all(grad_total)
    relation_out = relation.astype(jnp.float32) - LR_RELATION * grad_total
    return (left_block, holding, relation_out)


def solution(mesh):
    in_specs = (
        P(("group", "inner"), None),
        P(("group", "inner"), None),
        P(),
        P(("group", "inner"), None, None),
        P(("group", "inner"), None, None),
        P(("group", "inner"), None),
    )
    out_specs = (P(("group", "inner"), None), P(("group", "inner"), None), P())
    return jax.shard_map(shards, mesh=mesh, in_specs=in_specs, out_specs=out_specs, check_vma=False)
```

```python
import jax
import jax.numpy as jnp
from jax import lax
from jax.sharding import PartitionSpec as P

SCORE_SCALE = 0.1875
LR_EMBED = 0.5
LR_RELATION = 0.02
AXES = ("group", "inner")


def moved(value, mask):
    pairs = [(source, source ^ mask) for source in range(lax.axis_size("inner"))]
    return lax.ppermute(value, "inner", pairs)


def matmul(a, b, dims):
    return lax.dot_general(a, b, (dims, ((), ())), preferred_element_type=jnp.float32)


def summed_over_all(partial):
    rows, width = partial.shape
    pieces = partial.astype(jnp.bfloat16).reshape(rows, 2, width // 2)
    pieces = lax.all_to_all(pieces, AXES, 0, 0)
    own_row = jnp.sum(pieces.astype(jnp.float32), axis=0).astype(jnp.bfloat16)
    copies = jnp.broadcast_to(own_row[None], pieces.shape)
    gathered = lax.all_to_all(copies, AXES, 0, 0)
    return gathered.reshape(rows, width).astype(jnp.float32)


def source_table(src_row, rows):
    return (src_row[:, None] == jnp.arange(rows, dtype=jnp.int32)[None, :]).astype(jnp.bfloat16)


def picked_rows(left_block, table):
    return matmul(table, left_block, ((1,), (0,))).astype(jnp.bfloat16)


def edge_coeffs(picked, relation, holding, target):
    queries = matmul(picked, relation, ((1,), (0,))).astype(jnp.bfloat16)
    scores = matmul(queries, holding, ((1,), (1,))) * SCORE_SCALE
    maxima = jnp.max(scores, axis=1, keepdims=True)
    expos = jnp.exp(scores - maxima)
    softmax_w = expos / jnp.sum(expos, axis=1, keepdims=True)
    live_mask = (target >= 0).astype(jnp.float32)
    columns = jnp.arange(holding.shape[0], dtype=jnp.int32)
    onehot = (columns[None, :] == target[:, None]).astype(jnp.float32)
    coeffs = ((softmax_w - onehot) * live_mask[:, None]).astype(jnp.bfloat16)
    return queries, coeffs


def updated_holding(holding, coeffs, queries):
    held_grad = matmul(coeffs, queries, ((0,), (0,))) * SCORE_SCALE
    return (holding.astype(jnp.float32) - LR_EMBED * held_grad).astype(jnp.bfloat16)


def query_gradient(coeffs, holding):
    return (matmul(coeffs, holding, ((1,), (0,))) * SCORE_SCALE).astype(jnp.bfloat16)


def updated_left(left_block, table, query_grad, relation):
    summed_rows = matmul(table, query_grad, ((0,), (0,)))
    high = summed_rows.astype(jnp.bfloat16)
    low = (summed_rows - high.astype(jnp.float32)).astype(jnp.bfloat16)
    left_grad = matmul(high, relation, ((1,), (1,))) + matmul(low, relation, ((1,), (1,)))
    return (left_block.astype(jnp.float32) - LR_EMBED * left_grad).astype(jnp.bfloat16)


def shards(left_part, right_part, relation, src_index, dst_index, lengths):
    rows = left_part.shape[0]
    slots = jnp.arange(src_index.shape[2], dtype=jnp.int32)
    targets = jnp.where(slots[None, :] < lengths[0][:, None], dst_index[0], -1)
    tables = [source_table(src_index[0, meeting], rows) for meeting in range(4)]

    held = moved(right_part, 1)
    picked, targets = lax.optimization_barrier((picked_rows(left_part, tables[0]), targets))
    target1 = moved(targets[1], 2)
    target3 = moved(targets[3], 8)
    queries, coeffs = edge_coeffs(picked, relation, held, targets[0])
    query_grad = query_gradient(coeffs, held)
    left = updated_left(left_part, tables[0], query_grad, relation)
    relation_grad = matmul(picked, query_grad, ((0,), (0,)))
    held = updated_holding(held, coeffs, queries)

    picked = moved(picked_rows(left, tables[1]), 2)
    queries, coeffs = edge_coeffs(picked, relation, held, target1)
    new_held, coeffs = lax.optimization_barrier((updated_holding(held, coeffs, queries), coeffs))
    query_grad = query_gradient(coeffs, held)
    relation_grad = relation_grad + matmul(picked, query_grad, ((0,), (0,)))
    held = moved(new_held, 6)
    left = updated_left(left, tables[1], moved(query_grad, 2), relation)

    picked = picked_rows(left, tables[2])
    queries, coeffs = edge_coeffs(picked, relation, held, targets[2])
    query_grad = query_gradient(coeffs, held)
    left = updated_left(left, tables[2], query_grad, relation)
    relation_grad = relation_grad + matmul(picked, query_grad, ((0,), (0,)))
    held = updated_holding(held, coeffs, queries)

    picked = moved(picked_rows(left, tables[3]), 8)
    queries, coeffs = edge_coeffs(picked, relation, held, target3)
    query_grad = query_gradient(coeffs, held)
    relation_grad = relation_grad + matmul(picked, query_grad, ((0,), (0,)))
    relation_grad, query_grad = lax.optimization_barrier((relation_grad, query_grad))
    total = summed_over_all(relation_grad)
    held = moved(updated_holding(held, coeffs, queries), 8)
    left = updated_left(left, tables[3], moved(query_grad, 8), relation)

    relation_out = relation.astype(jnp.float32) - LR_RELATION * total
    return (left, held, relation_out)


def solution(mesh):
    in_specs = (
        P(AXES, None),
        P(AXES, None),
        P(),
        P(AXES, None, None),
        P(AXES, None, None),
        P(AXES, None),
    )
    out_specs = (P(AXES, None), P(AXES, None), P())
    return jax.shard_map(shards, mesh=mesh, in_specs=in_specs, out_specs=out_specs, check_vma=False)
```

```python
import functools
import jax
import jax.numpy as jnp
from jax import lax
from jax.experimental import pallas as pl
from jax.experimental.pallas import tpu as pltpu
from jax.sharding import PartitionSpec as P

SCORE_SCALE = 0.1875
LR_EMBED = 0.5
LR_RELATION = 0.02
EXP_SCALE = SCORE_SCALE * 1.4426950408889634
CODE_ROWS = 16
AXES = ("group", "inner")
VM = pltpu.VMEM
TE = 256


def dot(a, b, dims):
    return lax.dot_general(a, b, (dims, ((), ())), preferred_element_type=jnp.float32)


RC = 64


def fill_coeffs(queries, held_ref, target_ref, first, coeffs_ref, scores_ref):
    rows = held_ref.shape[0]
    edges = queries.shape[0]
    parts = [slice(start, start + TE) for start in range(0, edges, TE)]
    chunks = [slice(start, start + RC) for start in range(0, rows, RC)]
    fold = lambda value, op: functools.reduce(op, [value[k:k + 8] for k in range(0, value.shape[0], 8)])
    for part in parts:
        scores_ref[:, part] = dot(held_ref[...], queries[part], ((1,), (1,)))
    for part in parts:
        top = functools.reduce(jnp.maximum, [fold(scores_ref[c, part], jnp.maximum) for c in chunks])
        top = jnp.max(top, axis=0, keepdims=True)
        total = None
        for c in chunks:
            expos = jnp.exp2((scores_ref[c, part] - top) * EXP_SCALE)
            scores_ref[c, part] = expos
            folded = fold(expos, jnp.add)
            total = folded if total is None else total + folded
        high, low = first + part.start // TE, first + (edges + part.start) // TE
        target = target_ref[high:high + 1, :].astype(jnp.float32) * 32.0 + target_ref[low:low + 1, :].astype(jnp.float32)
        live = (target >= 0.0).astype(jnp.float32)
        weight = live / jnp.sum(total, axis=0, keepdims=True)
        ids = lax.broadcasted_iota(jnp.int32, (RC, TE), 0).astype(jnp.float32)
        for c in chunks:
            softmax_w = scores_ref[c, part] * weight
            coeffs = jnp.where(ids == target - float(c.start), softmax_w - 1.0, softmax_w)
            coeffs_ref[c, part] = coeffs.astype(jnp.bfloat16)


def gradient_of_queries(coeffs_ref, held_ref):
    return (dot(coeffs_ref[...], held_ref[...], ((0,), (0,))) * SCORE_SCALE).astype(jnp.bfloat16)


def local_kernel(meeting, queries_ref, held_ref, codes_ref, relation_ref, same_ref, base_ref, coeffs_ref, grad_ref, next_ref, scores_ref):
    edges = queries_ref.shape[0]
    fill_coeffs(queries_ref[...], held_ref, codes_ref, CODE_ROWS * meeting, coeffs_ref, scores_ref)
    grad = gradient_of_queries(coeffs_ref, held_ref)
    grad_ref[...] = grad
    row_grad = dot(grad, relation_ref[...], ((1,), (1,)))
    high = row_grad.astype(jnp.bfloat16)
    low = (row_grad - high.astype(jnp.float32)).astype(jnp.bfloat16)
    summed = dot(same_ref[...], high, ((1,), (0,))) + dot(same_ref[...], low, ((1,), (0,)))
    next_ref[edges:, :] = codes_ref[CODE_ROWS * (meeting + 1):CODE_ROWS * (meeting + 2), :]
    next_ref[:edges, :] = (base_ref[...].astype(jnp.float32) - LR_EMBED * summed).astype(jnp.bfloat16)


def held_kernel(picked_ref, held_ref, relation_ref, new_ref, coeffs_ref, scores_ref):
    edges = coeffs_ref.shape[1]
    queries = dot(picked_ref[:edges, :], relation_ref[...], ((1,), (0,))).astype(jnp.bfloat16)
    fill_coeffs(queries, held_ref, picked_ref, edges, coeffs_ref, scores_ref)
    held_grad = dot(coeffs_ref[...], queries, ((1,), (0,)))
    new_ref[...] = (held_ref[...].astype(jnp.float32) - (LR_EMBED * SCORE_SCALE) * held_grad).astype(jnp.bfloat16)


def last_kernel(picked_ref, held_ref, relation_ref, before_ref, pieces_ref, coeffs_ref, grad_ref, queries_ref, scores_ref):
    edges = coeffs_ref.shape[1]
    picked = picked_ref[:edges, :]
    queries = dot(picked, relation_ref[...], ((1,), (0,))).astype(jnp.bfloat16)
    queries_ref[...] = queries
    fill_coeffs(queries, held_ref, picked_ref, edges, coeffs_ref, scores_ref)
    grad = gradient_of_queries(coeffs_ref, held_ref)
    grad_ref[...] = grad
    total = before_ref[...] + dot(picked, grad, ((0,), (0,)))
    half = total.shape[1] // 2
    pieces_ref[:total.shape[0], :] = total[:, :half].astype(jnp.bfloat16)
    pieces_ref[total.shape[0]:, :] = total[:, half:].astype(jnp.bfloat16)


def sum_kernel(pieces_ref, copies_ref):
    pairs = [pieces_ref[k:k + 64, :].astype(jnp.float32) for k in range(0, pieces_ref.shape[0], 64)]
    total = functools.reduce(jnp.add, pairs)
    total = functools.reduce(jnp.add, [total[k:k + 8] for k in range(0, 64, 8)])
    first = total[0:1] + total[2:3] + total[4:5] + total[6:7]
    second = total[1:2] + total[3:4] + total[5:6] + total[7:8]
    parity = lax.broadcasted_iota(jnp.int32, (16, total.shape[1]), 0) % 2
    tile = jnp.where(parity == 0, first, second).astype(jnp.bfloat16)
    for k in range(0, copies_ref.shape[0], 16):
        copies_ref[k:k + 16, :] = tile


def finish_kernel(gathered_ref, relation_ref, out_ref):
    rows, width = out_ref.shape
    half = width // 2
    for k in range(2):
        columns = slice(k * half, (k + 1) * half)
        total = gathered_ref[k * rows:(k + 1) * rows, :].astype(jnp.float32)
        out_ref[:, columns] = relation_ref[:, columns].astype(jnp.float32) - LR_RELATION * total


def copy_kernel(source_ref, out_ref):
    out_ref[...] = source_ref[...]


def call(kernel, outs, *args, scratch=()):
    spec = pl.BlockSpec(memory_space=VM)
    return pl.pallas_call(
        kernel,
        out_shape=outs,
        in_specs=[spec] * len(args),
        out_specs=jax.tree.map(lambda _: spec, outs),
        scratch_shapes=list(scratch),
        compiler_params=pltpu.CompilerParams(vmem_limit_bytes=16 << 20),
    )(*args)


def vmem(*shape):
    return VM(shape, jnp.bfloat16)


def local_meeting(meeting, queries, held, codes, relation, same, base):
    (edges, width), rows = queries.shape, held.shape[0]
    outs = (vmem(rows, edges), vmem(edges, width), vmem(edges + CODE_ROWS, width))
    scratch = [VM((rows, edges), jnp.float32)]
    return call(functools.partial(local_kernel, meeting), outs, queries, held, codes, relation, same, base, scratch=scratch)


def held_meeting(picked, held, relation, edges):
    rows, width = held.shape
    outs = (vmem(rows, width), vmem(rows, edges))
    return call(held_kernel, outs, picked, held, relation, scratch=[VM((rows, edges), jnp.float32)])


def last_meeting(picked, held, relation, before, edges):
    rows, width = held.shape
    outs = (vmem(2 * width, width // 2), vmem(rows, edges), vmem(edges, width), vmem(edges, width))
    scratch = [VM((rows, edges), jnp.float32)]
    return call(last_kernel, outs, picked, held, relation, before, scratch=scratch)


def shared_sums(pieces):
    devices = lax.axis_size(AXES)
    rows, lanes = pieces.shape
    shape = (devices, rows // devices, lanes)
    pieces = lax.all_to_all(pieces.reshape(shape), AXES, 0, 0).reshape(rows, lanes)
    copies = call(sum_kernel, vmem(rows, lanes), pieces)
    return lax.all_to_all(copies.reshape(shape), AXES, 0, 0).reshape(rows, lanes)


def moved(value, mask):
    pairs = [(source, source ^ mask) for source in range(lax.axis_size("inner"))]
    return lax.ppermute(value, "inner", pairs)


def source_table(src_row, rows):
    return (src_row[:, None] == jnp.arange(rows, dtype=jnp.int32)[None, :]).astype(jnp.bfloat16)


def same_source(rows, columns):
    return (rows[:, None] == columns[None, :]).astype(jnp.bfloat16)


def picked_rows(left_block, table):
    return dot(table, left_block, ((1,), (0,))).astype(jnp.bfloat16)


def queries_of(picked, relation):
    return dot(picked, relation, ((1,), (0,))).astype(jnp.bfloat16)


def updated_holding(holding, coeffs, queries):
    held_grad = dot(coeffs, queries, ((1,), (0,)))
    return (holding.astype(jnp.float32) - (LR_EMBED * SCORE_SCALE) * held_grad).astype(jnp.bfloat16)


def query_gradient(coeffs, holding):
    return (dot(coeffs, holding, ((0,), (0,))) * SCORE_SCALE).astype(jnp.bfloat16)


def relation_gradient(picked, query_grad):
    return dot(picked, query_grad, ((0,), (0,)))


def updated_left(left_block, table, query_grad, relation):
    summed_rows = dot(table, query_grad, ((0,), (0,)))
    high = summed_rows.astype(jnp.bfloat16)
    low = (summed_rows - high.astype(jnp.float32)).astype(jnp.bfloat16)
    left_grad = dot(high, relation, ((1,), (1,))) + dot(low, relation, ((1,), (1,)))
    return (left_block.astype(jnp.float32) - LR_EMBED * left_grad).astype(jnp.bfloat16)


def coded(targets):
    meetings = targets.shape[0]
    lines = jnp.concatenate([targets // 32, targets % 32], axis=1).astype(jnp.bfloat16)
    lines = lines.reshape(meetings, -1, TE)
    lines = jnp.pad(lines, ((0, 0), (0, CODE_ROWS - lines.shape[1]), (0, 0)))
    return lines.reshape(meetings * CODE_ROWS, TE)


def shards(left_part, right_part, relation, src_index, dst_index, lengths):
    rows = left_part.shape[0]
    edges = src_index.shape[2]
    sources = src_index[0]

    held = moved(right_part, 1)
    slots = jnp.arange(edges, dtype=jnp.int32)
    targets = jnp.where(slots[None, :] < lengths[0][:, None], dst_index[0], -1)
    codes = coded(targets)
    tables = [source_table(sources[meeting], rows) for meeting in range(4)]
    picked0 = picked_rows(left_part, tables[0])
    queries0 = queries_of(picked0, relation)
    base = picked_rows(left_part, tables[1])
    same = same_source(sources[1], sources[0])
    coeffs, query_grad, picked1 = local_meeting(0, queries0, held, codes, relation, same, base)

    rows1 = moved(picked1, 2)
    held = updated_holding(held, coeffs, queries0)
    left = updated_left(left_part, tables[0], query_grad, relation)
    relation_grad = relation_gradient(picked0, query_grad)
    new_held, coeffs = held_meeting(rows1, held, relation, edges)
    arriving = moved(new_held, 6)
    query_grad = query_gradient(coeffs, held)
    relation_grad = relation_grad + relation_gradient(rows1[:edges], query_grad)
    left = updated_left(left, tables[1], moved(query_grad, 2), relation)

    held = arriving
    picked2 = picked_rows(left, tables[2])
    queries2 = queries_of(picked2, relation)
    base = picked_rows(left, tables[3])
    same = same_source(sources[3], sources[2])
    coeffs, query_grad, picked3 = local_meeting(2, queries2, held, codes, relation, same, base)

    rows3 = moved(picked3, 8)
    held = updated_holding(held, coeffs, queries2)
    left = updated_left(left, tables[2], query_grad, relation)
    relation_grad = relation_grad + relation_gradient(picked2, query_grad)
    pieces, coeffs, query_grad, queries3 = last_meeting(rows3, held, relation, relation_grad, edges)
    sums = shared_sums(pieces)
    held = moved(updated_holding(held, coeffs, queries3), 8)
    left = updated_left(left, tables[3], moved(query_grad, 8), relation)
    held = call(copy_kernel, jax.ShapeDtypeStruct(held.shape, held.dtype), held)
    relation, held, left = lax.optimization_barrier((relation, held, left))
    relation_out = call(finish_kernel, jax.ShapeDtypeStruct(relation.shape, jnp.float32), sums, relation)
    return (left, held, relation_out)


def solution(mesh):
    in_specs = (
        P(AXES, None),
        P(AXES, None),
        P(),
        P(AXES, None, None),
        P(AXES, None, None),
        P(AXES, None),
    )
    out_specs = (P(AXES, None), P(AXES, None), P())
    return jax.shard_map(shards, mesh=mesh, in_specs=in_specs, out_specs=out_specs, check_vma=False)
```

```python
import functools
import jax
import jax.numpy as jnp
from jax import lax
from jax.experimental import pallas as pl
from jax.experimental.pallas import tpu as pltpu
from jax.sharding import PartitionSpec as P

SCORE_SCALE = 0.1875
LR_EMBED = 0.5
LR_RELATION = 0.02
EXP_SCALE = SCORE_SCALE * 1.4426950408889634
CODE_ROWS = 16
AXES = ("group", "inner")
VM = pltpu.VMEM
TE = 256


def dot(a, b, dims):
    return lax.dot_general(a, b, (dims, ((), ())), preferred_element_type=jnp.float32)


RC = 64


def fill_coeffs(queries, held_ref, target_ref, first, coeffs_ref, scores_ref):
    rows = held_ref.shape[0]
    edges = queries.shape[0]
    parts = [slice(start, start + TE) for start in range(0, edges, TE)]
    chunks = [slice(start, start + RC) for start in range(0, rows, RC)]
    fold = lambda value, op: functools.reduce(op, [value[k:k + 8] for k in range(0, value.shape[0], 8)])
    for part in parts:
        scores_ref[:, part] = dot(held_ref[...], queries[part], ((1,), (1,)))
    for part in parts:
        top = functools.reduce(jnp.maximum, [fold(scores_ref[c, part], jnp.maximum) for c in chunks])
        top = jnp.max(top, axis=0, keepdims=True)
        total = None
        for c in chunks:
            expos = jnp.exp2((scores_ref[c, part] - top) * EXP_SCALE)
            scores_ref[c, part] = expos
            folded = fold(expos, jnp.add)
            total = folded if total is None else total + folded
        high, low = first + part.start // TE, first + (edges + part.start) // TE
        target = target_ref[high:high + 1, :].astype(jnp.float32) * 32.0 + target_ref[low:low + 1, :].astype(jnp.float32)
        live = (target >= 0.0).astype(jnp.float32)
        weight = live / jnp.sum(total, axis=0, keepdims=True)
        ids = lax.broadcasted_iota(jnp.int32, (RC, TE), 0).astype(jnp.float32)
        for c in chunks:
            softmax_w = scores_ref[c, part] * weight
            coeffs = jnp.where(ids == target - float(c.start), softmax_w - 1.0, softmax_w)
            coeffs_ref[c, part] = coeffs.astype(jnp.bfloat16)


def gradient_of_queries(coeffs_ref, held_ref):
    return (dot(coeffs_ref[...], held_ref[...], ((0,), (0,))) * SCORE_SCALE).astype(jnp.bfloat16)


def local_kernel(meeting, queries_ref, held_ref, codes_ref, relation_ref, same_ref, base_ref, coeffs_ref, grad_ref, next_ref, scores_ref):
    edges = queries_ref.shape[0]
    fill_coeffs(queries_ref[...], held_ref, codes_ref, CODE_ROWS * meeting, coeffs_ref, scores_ref)
    grad = gradient_of_queries(coeffs_ref, held_ref)
    grad_ref[...] = grad
    row_grad = dot(grad, relation_ref[...], ((1,), (1,)))
    high = row_grad.astype(jnp.bfloat16)
    low = (row_grad - high.astype(jnp.float32)).astype(jnp.bfloat16)
    summed = dot(same_ref[...], high, ((1,), (0,))) + dot(same_ref[...], low, ((1,), (0,)))
    next_ref[edges:, :] = codes_ref[CODE_ROWS * (meeting + 1):CODE_ROWS * (meeting + 2), :]
    next_ref[:edges, :] = (base_ref[...].astype(jnp.float32) - LR_EMBED * summed).astype(jnp.bfloat16)


def held_kernel(picked_ref, held_ref, relation_ref, new_ref, coeffs_ref, scores_ref):
    edges = coeffs_ref.shape[1]
    queries = dot(picked_ref[:edges, :], relation_ref[...], ((1,), (0,))).astype(jnp.bfloat16)
    fill_coeffs(queries, held_ref, picked_ref, edges, coeffs_ref, scores_ref)
    held_grad = dot(coeffs_ref[...], queries, ((1,), (0,)))
    new_ref[...] = (held_ref[...].astype(jnp.float32) - (LR_EMBED * SCORE_SCALE) * held_grad).astype(jnp.bfloat16)


def last_kernel(picked_ref, held_ref, relation_ref, before_ref, pieces_ref, coeffs_ref, grad_ref, queries_ref, scores_ref):
    edges = coeffs_ref.shape[1]
    picked = picked_ref[:edges, :]
    queries = dot(picked, relation_ref[...], ((1,), (0,))).astype(jnp.bfloat16)
    queries_ref[...] = queries
    fill_coeffs(queries, held_ref, picked_ref, edges, coeffs_ref, scores_ref)
    grad = gradient_of_queries(coeffs_ref, held_ref)
    grad_ref[...] = grad
    total = before_ref[...] + dot(picked, grad, ((0,), (0,)))
    half = total.shape[1] // 2
    pieces_ref[:total.shape[0], :] = total[:, :half].astype(jnp.bfloat16)
    pieces_ref[total.shape[0]:, :] = total[:, half:].astype(jnp.bfloat16)


def sum_kernel(pieces_ref, copies_ref):
    lines = CODE_ROWS
    parts = [pieces_ref[k:k + lines, :].astype(jnp.float32) for k in range(0, pieces_ref.shape[0], lines)]
    total = functools.reduce(jnp.add, parts).astype(jnp.bfloat16)
    for k in range(0, copies_ref.shape[0], lines):
        copies_ref[k:k + lines, :] = total


def finish_kernel(gathered_ref, relation_ref, out_ref):
    rows, width = out_ref.shape
    half = width // 2
    for k in range(2):
        columns = slice(k * half, (k + 1) * half)
        total = gathered_ref[k * rows:(k + 1) * rows, :].astype(jnp.float32)
        out_ref[:, columns] = relation_ref[:, columns].astype(jnp.float32) - LR_RELATION * total


def copy_kernel(source_ref, out_ref):
    out_ref[...] = source_ref[...]


def call(kernel, outs, *args, scratch=()):
    spec = pl.BlockSpec(memory_space=VM)
    return pl.pallas_call(
        kernel,
        out_shape=outs,
        in_specs=[spec] * len(args),
        out_specs=jax.tree.map(lambda _: spec, outs),
        scratch_shapes=list(scratch),
        compiler_params=pltpu.CompilerParams(vmem_limit_bytes=16 << 20),
    )(*args)


def vmem(*shape):
    return VM(shape, jnp.bfloat16)


def local_meeting(meeting, queries, held, codes, relation, same, base):
    (edges, width), rows = queries.shape, held.shape[0]
    outs = (vmem(rows, edges), vmem(edges, width), vmem(edges + CODE_ROWS, width))
    scratch = [VM((rows, edges), jnp.float32)]
    return call(functools.partial(local_kernel, meeting), outs, queries, held, codes, relation, same, base, scratch=scratch)


def held_meeting(picked, held, relation, edges):
    rows, width = held.shape
    outs = (vmem(rows, width), vmem(rows, edges))
    return call(held_kernel, outs, picked, held, relation, scratch=[VM((rows, edges), jnp.float32)])


def last_meeting(picked, held, relation, before, edges):
    rows, width = held.shape
    outs = (vmem(2 * width, width // 2), vmem(rows, edges), vmem(edges, width), vmem(edges, width))
    scratch = [VM((rows, edges), jnp.float32)]
    return call(last_kernel, outs, picked, held, relation, before, scratch=scratch)


def exchanged(pieces, axes, groups):
    rows, lanes = pieces.shape
    pieces = pieces.reshape(len(groups[0]), -1, lanes)
    return lax.all_to_all(pieces, axes, 0, 0, axis_index_groups=groups).reshape(rows, lanes)


def shared_sums(pieces):
    n_group, n_inner = lax.axis_size("group"), lax.axis_size("inner")
    depth = 8
    columns = range(n_inner // depth)
    planes = [[g * n_inner + x * depth + z for g in range(n_group) for x in columns] for z in range(depth)]
    lines = [[x * depth + z for z in range(depth)] for x in columns]
    rows, lanes = pieces.shape
    pieces = exchanged(pieces, AXES, planes)
    copies = call(sum_kernel, vmem(depth * CODE_ROWS, lanes), pieces)
    copies = call(sum_kernel, vmem(rows, lanes), exchanged(copies, "inner", lines))
    return exchanged(copies, AXES, planes)


def moved(value, mask):
    pairs = [(source, source ^ mask) for source in range(lax.axis_size("inner"))]
    return lax.ppermute(value, "inner", pairs)


def source_table(src_row, rows):
    return (src_row[:, None] == jnp.arange(rows, dtype=jnp.int32)[None, :]).astype(jnp.bfloat16)


def same_source(rows, columns):
    return (rows[:, None] == columns[None, :]).astype(jnp.bfloat16)


def picked_rows(left_block, table):
    return dot(table, left_block, ((1,), (0,))).astype(jnp.bfloat16)


def queries_of(picked, relation):
    return dot(picked, relation, ((1,), (0,))).astype(jnp.bfloat16)


def updated_holding(holding, coeffs, queries):
    held_grad = dot(coeffs, queries, ((1,), (0,)))
    return (holding.astype(jnp.float32) - (LR_EMBED * SCORE_SCALE) * held_grad).astype(jnp.bfloat16)


def query_gradient(coeffs, holding):
    return (dot(coeffs, holding, ((0,), (0,))) * SCORE_SCALE).astype(jnp.bfloat16)


def relation_gradient(picked, query_grad):
    return dot(picked, query_grad, ((0,), (0,)))


def updated_left(left_block, table, query_grad, relation):
    summed_rows = dot(table, query_grad, ((0,), (0,)))
    high = summed_rows.astype(jnp.bfloat16)
    low = (summed_rows - high.astype(jnp.float32)).astype(jnp.bfloat16)
    left_grad = dot(high, relation, ((1,), (1,))) + dot(low, relation, ((1,), (1,)))
    return (left_block.astype(jnp.float32) - LR_EMBED * left_grad).astype(jnp.bfloat16)


def coded(targets):
    meetings = targets.shape[0]
    lines = jnp.concatenate([targets // 32, targets % 32], axis=1).astype(jnp.bfloat16)
    lines = lines.reshape(meetings, -1, TE)
    lines = jnp.pad(lines, ((0, 0), (0, CODE_ROWS - lines.shape[1]), (0, 0)))
    return lines.reshape(meetings * CODE_ROWS, TE)


def shards(left_part, right_part, relation, src_index, dst_index, lengths):
    rows = left_part.shape[0]
    edges = src_index.shape[2]
    sources = src_index[0]

    held = moved(right_part, 1)
    slots = jnp.arange(edges, dtype=jnp.int32)
    targets = jnp.where(slots[None, :] < lengths[0][:, None], dst_index[0], -1)
    codes = coded(targets)
    tables = [source_table(sources[meeting], rows) for meeting in range(4)]
    picked0 = picked_rows(left_part, tables[0])
    queries0 = queries_of(picked0, relation)
    base = picked_rows(left_part, tables[1])
    same = same_source(sources[1], sources[0])
    coeffs, query_grad, picked1 = local_meeting(0, queries0, held, codes, relation, same, base)

    rows1 = moved(picked1, 2)
    held = updated_holding(held, coeffs, queries0)
    left = updated_left(left_part, tables[0], query_grad, relation)
    relation_grad = relation_gradient(picked0, query_grad)
    new_held, coeffs = held_meeting(rows1, held, relation, edges)
    arriving = moved(new_held, 6)
    query_grad = query_gradient(coeffs, held)
    relation_grad = relation_grad + relation_gradient(rows1[:edges], query_grad)
    left = updated_left(left, tables[1], moved(query_grad, 2), relation)

    held = arriving
    picked2 = picked_rows(left, tables[2])
    queries2 = queries_of(picked2, relation)
    base = picked_rows(left, tables[3])
    same = same_source(sources[3], sources[2])
    coeffs, query_grad, picked3 = local_meeting(2, queries2, held, codes, relation, same, base)

    rows3 = moved(picked3, 8)
    held = updated_holding(held, coeffs, queries2)
    left = updated_left(left, tables[2], query_grad, relation)
    relation_grad = relation_grad + relation_gradient(picked2, query_grad)
    pieces, coeffs, query_grad, queries3 = last_meeting(rows3, held, relation, relation_grad, edges)
    sums = shared_sums(pieces)
    held = moved(updated_holding(held, coeffs, queries3), 8)
    left = updated_left(left, tables[3], moved(query_grad, 8), relation)
    held = call(copy_kernel, jax.ShapeDtypeStruct(held.shape, held.dtype), held)
    relation, held, left = lax.optimization_barrier((relation, held, left))
    relation_out = call(finish_kernel, jax.ShapeDtypeStruct(relation.shape, jnp.float32), sums, relation)
    return (left, held, relation_out)


def solution(mesh):
    in_specs = (
        P(AXES, None),
        P(AXES, None),
        P(),
        P(AXES, None, None),
        P(AXES, None, None),
        P(AXES, None),
    )
    out_specs = (P(AXES, None), P(AXES, None), P())
    return jax.shard_map(shards, mesh=mesh, in_specs=in_specs, out_specs=out_specs, check_vma=False)
```

```python
import functools
import jax
import jax.numpy as jnp
from jax import lax
from jax.experimental import pallas as pl
from jax.experimental.pallas import tpu as pltpu
from jax.sharding import PartitionSpec as P

SCORE_SCALE = 0.1875
LR_EMBED = 0.5
LR_RELATION = 0.02
EXP_SCALE = SCORE_SCALE * 1.4426950408889634
CODE_ROWS = 16
AXES = ("group", "inner")
VM = pltpu.VMEM
TE = 256


def dot(a, b, dims):
    return lax.dot_general(a, b, (dims, ((), ())), preferred_element_type=jnp.float32)


RC = 128


def scores_of(queries, held_ref, scores_ref, part):
    scores_ref[:, part] = dot(held_ref[...], queries[part], ((1,), (1,)))


def fill_coeffs(codes_ref, first, coeffs_ref, scores_ref, part):
    rows, edges = coeffs_ref.shape
    chunks = [slice(start, start + RC) for start in range(0, rows, RC)]
    fold = lambda value, op: functools.reduce(op, [value[k:k + 8] for k in range(0, value.shape[0], 8)])
    top = functools.reduce(jnp.maximum, [fold(scores_ref[c, part], jnp.maximum) for c in chunks])
    top = jnp.max(top, axis=0, keepdims=True)
    total = None
    for c in chunks:
        expos = jnp.exp2((scores_ref[c, part] - top) * EXP_SCALE)
        scores_ref[c, part] = expos
        folded = fold(expos, jnp.add)
        total = folded if total is None else total + folded
    high, low = first + part.start // TE, first + (edges + part.start) // TE
    target = codes_ref[high:high + 1, :].astype(jnp.float32) * 32.0 + codes_ref[low:low + 1, :].astype(jnp.float32)
    live = (target >= 0.0).astype(jnp.float32)
    weight = live / jnp.sum(total, axis=0, keepdims=True)
    ids = lax.broadcasted_iota(jnp.int32, (RC, TE), 0).astype(jnp.float32)
    for c in chunks:
        softmax_w = scores_ref[c, part] * weight
        coeffs = jnp.where(ids == target - float(c.start), softmax_w - 1.0, softmax_w)
        coeffs_ref[c, part] = coeffs.astype(jnp.bfloat16)


def parts_of(edges):
    return [slice(start, start + TE) for start in range(0, edges, TE)]


def fill_gradient(coeffs_ref, held_ref, grad_ref, part):
    grad = dot(coeffs_ref[:, part], held_ref[...], ((0,), (0,))) * SCORE_SCALE
    grad_ref[part, :] = grad.astype(jnp.bfloat16)


def meeting_body(queries, held_ref, codes_ref, first, coeffs_ref, scores_ref, then):
    parts = parts_of(coeffs_ref.shape[1])
    scores_of(queries, held_ref, scores_ref, parts[0])
    for k, part in enumerate(parts):
        if k + 1 < len(parts):
            scores_of(queries, held_ref, scores_ref, parts[k + 1])
        fill_coeffs(codes_ref, first, coeffs_ref, scores_ref, part)
        then(part)


def local_kernel(meeting, queries_ref, held_ref, codes_ref, relation_ref, same_ref, base_ref, coeffs_ref, grad_ref, next_ref, scores_ref):
    edges = queries_ref.shape[0]
    then = lambda part: fill_gradient(coeffs_ref, held_ref, grad_ref, part)
    meeting_body(queries_ref[...], held_ref, codes_ref, CODE_ROWS * meeting, coeffs_ref, scores_ref, then)
    summed = dot(same_ref[...], grad_ref[...], ((1,), (0,)))
    high = summed.astype(jnp.bfloat16)
    low = (summed - high.astype(jnp.float32)).astype(jnp.bfloat16)
    change = dot(high, relation_ref[...], ((1,), (1,))) + dot(low, relation_ref[...], ((1,), (1,)))
    next_ref[edges:, :] = codes_ref[CODE_ROWS * (meeting + 1):CODE_ROWS * (meeting + 2), :]
    next_ref[:edges, :] = (base_ref[...].astype(jnp.float32) - LR_EMBED * change).astype(jnp.bfloat16)


def held_kernel(picked_ref, held_ref, relation_ref, new_ref, coeffs_ref, scores_ref):
    edges = coeffs_ref.shape[1]
    queries = dot(picked_ref[:edges, :], relation_ref[...], ((1,), (0,))).astype(jnp.bfloat16)
    meeting_body(queries, held_ref, picked_ref, edges, coeffs_ref, scores_ref, lambda part: None)
    held_grad = dot(coeffs_ref[...], queries, ((1,), (0,)))
    new_ref[...] = (held_ref[...].astype(jnp.float32) - (LR_EMBED * SCORE_SCALE) * held_grad).astype(jnp.bfloat16)


def last_kernel(picked_ref, held_ref, relation_ref, before_ref, pieces_ref, coeffs_ref, grad_ref, queries_ref, scores_ref):
    edges = coeffs_ref.shape[1]
    picked = picked_ref[:edges, :]
    queries = dot(picked, relation_ref[...], ((1,), (0,))).astype(jnp.bfloat16)
    queries_ref[...] = queries
    then = lambda part: fill_gradient(coeffs_ref, held_ref, grad_ref, part)
    meeting_body(queries, held_ref, picked_ref, edges, coeffs_ref, scores_ref, then)
    total = before_ref[...] + dot(picked, grad_ref[...], ((0,), (0,)))
    half = total.shape[1] // 2
    pieces_ref[:total.shape[0], :] = total[:, :half].astype(jnp.bfloat16)
    pieces_ref[total.shape[0]:, :] = total[:, half:].astype(jnp.bfloat16)


def left_kernel(left_ref, source_ref, grad_ref, relation_ref, out_ref):
    rows = left_ref.shape[0]
    for start in range(0, rows, TE):
        part = slice(start, start + TE)
        ids = lax.broadcasted_iota(jnp.int32, (TE, source_ref.shape[1]), 0) + start
        table = (ids == source_ref[...]).astype(jnp.float32).astype(jnp.bfloat16)
        summed = dot(table, grad_ref[...], ((1,), (0,)))
        high = summed.astype(jnp.bfloat16)
        low = (summed - high.astype(jnp.float32)).astype(jnp.bfloat16)
        change = dot(high, relation_ref[...], ((1,), (1,))) + dot(low, relation_ref[...], ((1,), (1,)))
        out_ref[part, :] = (left_ref[part, :].astype(jnp.float32) - LR_EMBED * change).astype(jnp.bfloat16)


def sum_kernel(pieces_ref, copies_ref):
    lines = CODE_ROWS
    parts = [pieces_ref[k:k + lines, :].astype(jnp.float32) for k in range(0, pieces_ref.shape[0], lines)]
    total = functools.reduce(jnp.add, parts).astype(jnp.bfloat16)
    for k in range(0, copies_ref.shape[0], lines):
        copies_ref[k:k + lines, :] = total


def finish_kernel(gathered_ref, relation_ref, out_ref):
    rows, width = out_ref.shape
    half = width // 2
    for k in range(2):
        columns = slice(k * half, (k + 1) * half)
        total = gathered_ref[k * rows:(k + 1) * rows, :].astype(jnp.float32)
        out_ref[:, columns] = relation_ref[:, columns].astype(jnp.float32) - LR_RELATION * total


def copy_kernel(source_ref, out_ref):
    out_ref[...] = source_ref[...]


def call(kernel, outs, *args, scratch=()):
    spec = pl.BlockSpec(memory_space=VM)
    return pl.pallas_call(
        kernel,
        out_shape=outs,
        in_specs=[spec] * len(args),
        out_specs=jax.tree.map(lambda _: spec, outs),
        scratch_shapes=list(scratch),
        compiler_params=pltpu.CompilerParams(vmem_limit_bytes=16 << 20),
    )(*args)


def vmem(*shape):
    return VM(shape, jnp.bfloat16)


def local_meeting(meeting, queries, held, codes, relation, same, base):
    (edges, width), rows = queries.shape, held.shape[0]
    outs = (vmem(rows, edges), vmem(edges, width), vmem(edges + CODE_ROWS, width))
    scratch = [VM((rows, edges), jnp.float32)]
    return call(functools.partial(local_kernel, meeting), outs, queries, held, codes, relation, same, base, scratch=scratch)


def held_meeting(picked, held, relation, edges):
    rows, width = held.shape
    outs = (vmem(rows, width), vmem(rows, edges))
    return call(held_kernel, outs, picked, held, relation, scratch=[VM((rows, edges), jnp.float32)])


def last_meeting(picked, held, relation, before, edges):
    rows, width = held.shape
    outs = (vmem(2 * width, width // 2), vmem(rows, edges), vmem(edges, width), vmem(edges, width))
    scratch = [VM((rows, edges), jnp.float32)]
    return call(last_kernel, outs, picked, held, relation, before, scratch=scratch)


def exchanged(pieces, axes, groups):
    rows, lanes = pieces.shape
    pieces = pieces.reshape(len(groups[0]), -1, lanes)
    return lax.all_to_all(pieces, axes, 0, 0, axis_index_groups=groups).reshape(rows, lanes)


def shared_sums(pieces):
    n_group, n_inner = lax.axis_size("group"), lax.axis_size("inner")
    depth = 8
    columns = range(n_inner // depth)
    planes = [[g * n_inner + x * depth + z for g in range(n_group) for x in columns] for z in range(depth)]
    lines = [[x * depth + z for z in range(depth)] for x in columns]
    rows, lanes = pieces.shape
    pieces = exchanged(pieces, AXES, planes)
    copies = call(sum_kernel, vmem(depth * CODE_ROWS, lanes), pieces)
    copies = call(sum_kernel, vmem(rows, lanes), exchanged(copies, "inner", lines))
    return exchanged(copies, AXES, planes)


def moved(value, mask):
    pairs = [(source, source ^ mask) for source in range(lax.axis_size("inner"))]
    return lax.ppermute(value, "inner", pairs)


def source_table(src_row, rows):
    return (src_row[:, None] == jnp.arange(rows, dtype=jnp.int32)[None, :]).astype(jnp.bfloat16)


def same_source(rows, columns):
    return (rows[:, None] == columns[None, :]).astype(jnp.bfloat16)


def picked_rows(left_block, table):
    return dot(table, left_block, ((1,), (0,))).astype(jnp.bfloat16)


def queries_of(picked, relation):
    return dot(picked, relation, ((1,), (0,))).astype(jnp.bfloat16)


def updated_holding(holding, coeffs, queries):
    held_grad = dot(coeffs, queries, ((1,), (0,)))
    return (holding.astype(jnp.float32) - (LR_EMBED * SCORE_SCALE) * held_grad).astype(jnp.bfloat16)


def query_gradient(coeffs, holding):
    return (dot(coeffs, holding, ((0,), (0,))) * SCORE_SCALE).astype(jnp.bfloat16)


def relation_gradient(picked, query_grad):
    return dot(picked, query_grad, ((0,), (0,)))


def updated_left(left_block, source, query_grad, relation, out):
    return call(left_kernel, out, left_block, source.reshape(1, -1), query_grad, relation)


def coded(targets):
    meetings = targets.shape[0]
    lines = jnp.concatenate([targets // 32, targets % 32], axis=1).astype(jnp.bfloat16)
    lines = lines.reshape(meetings, -1, TE)
    lines = jnp.pad(lines, ((0, 0), (0, CODE_ROWS - lines.shape[1]), (0, 0)))
    return lines.reshape(meetings * CODE_ROWS, TE)


def shards(left_part, right_part, relation, src_index, dst_index, lengths):
    rows = left_part.shape[0]
    edges = src_index.shape[2]
    sources = src_index[0]

    held = moved(right_part, 1)
    slots = jnp.arange(edges, dtype=jnp.int32)
    targets = jnp.where(slots[None, :] < lengths[0][:, None], dst_index[0], -1)
    codes = coded(targets)
    tables = [source_table(sources[meeting], rows) for meeting in range(4)]
    picked0 = picked_rows(left_part, tables[0])
    queries0 = queries_of(picked0, relation)
    base = picked_rows(left_part, tables[1])
    same = same_source(sources[1], sources[0])
    coeffs, query_grad, picked1 = local_meeting(0, queries0, held, codes, relation, same, base)

    rows1 = moved(picked1, 2)
    held = updated_holding(held, coeffs, queries0)
    left = updated_left(left_part, sources[0], query_grad, relation, vmem(*left_part.shape))
    relation_grad = relation_gradient(picked0, query_grad)
    new_held, coeffs = held_meeting(rows1, held, relation, edges)
    arriving = moved(new_held, 6)
    query_grad = query_gradient(coeffs, held)
    relation_grad = relation_grad + relation_gradient(rows1[:edges], query_grad)
    left = updated_left(left, sources[1], moved(query_grad, 2), relation, vmem(*left.shape))

    held = arriving
    picked2 = picked_rows(left, tables[2])
    queries2 = queries_of(picked2, relation)
    base = picked_rows(left, tables[3])
    same = same_source(sources[3], sources[2])
    coeffs, query_grad, picked3 = local_meeting(2, queries2, held, codes, relation, same, base)

    rows3 = moved(picked3, 8)
    held = updated_holding(held, coeffs, queries2)
    left = updated_left(left, sources[2], query_grad, relation, vmem(*left.shape))
    relation_grad = relation_grad + relation_gradient(picked2, query_grad)
    pieces, coeffs, query_grad, queries3 = last_meeting(rows3, held, relation, relation_grad, edges)
    sums = shared_sums(pieces)
    held = updated_holding(held, coeffs, queries3)
    held = moved(held, 8)
    last = jax.ShapeDtypeStruct(left.shape, left.dtype)
    left = updated_left(left, sources[3], moved(query_grad, 8), relation, last)
    held = call(copy_kernel, jax.ShapeDtypeStruct(held.shape, held.dtype), held)
    relation, held, left = lax.optimization_barrier((relation, held, left))
    relation_out = call(finish_kernel, jax.ShapeDtypeStruct(relation.shape, jnp.float32), sums, relation)
    return (left, held, relation_out)


def solution(mesh):
    in_specs = (
        P(AXES, None),
        P(AXES, None),
        P(),
        P(AXES, None, None),
        P(AXES, None, None),
        P(AXES, None),
    )
    out_specs = (P(AXES, None), P(AXES, None), P())
    return jax.shard_map(shards, mesh=mesh, in_specs=in_specs, out_specs=out_specs, check_vma=False)
```

```python
import functools
import jax
import jax.numpy as jnp
from jax import lax
from jax.experimental import pallas as pl
from jax.experimental.pallas import tpu as pltpu
from jax.sharding import PartitionSpec as P

SCORE_SCALE = 0.1875
LR_EMBED = 0.5
LR_RELATION = 0.02
EXP_SCALE = SCORE_SCALE * 1.4426950408889634
CODE_ROWS = 16
AXES = ("group", "inner")
VM = pltpu.VMEM
TE = 256


def dot(a, b, dims):
    return lax.dot_general(a, b, (dims, ((), ())), preferred_element_type=jnp.float32)


RC = 128


def scores_of(queries, held_ref, scores_ref, part):
    scores_ref[:, part] = dot(held_ref[...], queries[part], ((1,), (1,)))


def fill_coeffs(codes_ref, high, low, coeffs_ref, scores_ref, part):
    rows = coeffs_ref.shape[0]
    chunks = [slice(start, start + RC) for start in range(0, rows, RC)]
    fold = lambda value, op: functools.reduce(op, [value[k:k + 8] for k in range(0, value.shape[0], 8)])
    top = functools.reduce(jnp.maximum, [fold(scores_ref[c, part], jnp.maximum) for c in chunks])
    top = jnp.max(top, axis=0, keepdims=True)
    total = None
    for c in chunks:
        expos = jnp.exp2((scores_ref[c, part] - top) * EXP_SCALE)
        scores_ref[c, part] = expos
        folded = fold(expos, jnp.add)
        total = folded if total is None else total + folded
    target = codes_ref[high:high + 1, :].astype(jnp.float32) * 32.0 + codes_ref[low:low + 1, :].astype(jnp.float32)
    live = (target >= 0.0).astype(jnp.float32)
    weight = live / jnp.sum(total, axis=0, keepdims=True)
    ids = lax.broadcasted_iota(jnp.int32, (RC, TE), 0).astype(jnp.float32)
    for c in chunks:
        softmax_w = scores_ref[c, part] * weight
        coeffs = jnp.where(ids == target - float(c.start), softmax_w - 1.0, softmax_w)
        coeffs_ref[c, part] = coeffs.astype(jnp.bfloat16)


def fill_gradient(coeffs_ref, held_ref, grad_ref, part):
    grad = dot(coeffs_ref[:, part], held_ref[...], ((0,), (0,))) * SCORE_SCALE
    grad_ref[part, :] = grad.astype(jnp.bfloat16)


def local_kernel(meeting, queries_ref, held_ref, codes_ref, relation_ref, same_ref, base_ref, coeffs_ref, grad_ref, first_ref, second_ref, scores_ref):
    edges = queries_ref.shape[0]
    parts = [slice(start, start + TE) for start in range(0, edges, TE)]
    code = CODE_ROWS * meeting
    scores_of(queries_ref[...], held_ref, scores_ref, parts[0])
    for k, part in enumerate(parts):
        if k + 1 < len(parts):
            scores_of(queries_ref[...], held_ref, scores_ref, parts[k + 1])
        fill_coeffs(codes_ref, code + k, code + len(parts) + k, coeffs_ref, scores_ref, part)
        fill_gradient(coeffs_ref, held_ref, grad_ref, part)
    for part, next_ref in zip(parts, (first_ref, second_ref)):
        summed = dot(same_ref[part, :], grad_ref[...], ((1,), (0,)))
        high = summed.astype(jnp.bfloat16)
        low = (summed - high.astype(jnp.float32)).astype(jnp.bfloat16)
        change = dot(high, relation_ref[...], ((1,), (1,))) + dot(low, relation_ref[...], ((1,), (1,)))
        next_ref[TE:, :] = codes_ref[code + CODE_ROWS:code + 2 * CODE_ROWS, :]
        next_ref[:TE, :] = (base_ref[part, :].astype(jnp.float32) - LR_EMBED * change).astype(jnp.bfloat16)


def half_of_meeting(half, picked_ref, held_ref, relation_ref, coeffs_ref, scores_ref):
    queries = dot(picked_ref[:TE, :], relation_ref[...], ((1,), (0,))).astype(jnp.bfloat16)
    part = slice(0, TE)
    scores_of(queries, held_ref, scores_ref, part)
    fill_coeffs(picked_ref, TE + half, TE + 2 + half, coeffs_ref, scores_ref, part)
    return queries


def first_kernel(picked_ref, held_ref, relation_ref, before_ref, coeffs_ref, queries_ref, grad_ref, after_ref, scores_ref):
    queries_ref[...] = half_of_meeting(0, picked_ref, held_ref, relation_ref, coeffs_ref, scores_ref)
    fill_gradient(coeffs_ref, held_ref, grad_ref, slice(0, TE))
    after_ref[...] = before_ref[...] + dot(picked_ref[:TE, :], grad_ref[...], ((0,), (0,)))


def held_kernel(picked_ref, held_ref, relation_ref, coeffs0_ref, queries0_ref, new_ref, coeffs_ref, scores_ref):
    queries = half_of_meeting(1, picked_ref, held_ref, relation_ref, coeffs_ref, scores_ref)
    held_grad = dot(coeffs0_ref[...], queries0_ref[...], ((1,), (0,))) + dot(coeffs_ref[...], queries, ((1,), (0,)))
    new_ref[...] = (held_ref[...].astype(jnp.float32) - (LR_EMBED * SCORE_SCALE) * held_grad).astype(jnp.bfloat16)


def last_kernel(picked_ref, held_ref, relation_ref, before_ref, pieces_ref, coeffs_ref, grad_ref, queries_ref, scores_ref):
    queries_ref[...] = half_of_meeting(1, picked_ref, held_ref, relation_ref, coeffs_ref, scores_ref)
    fill_gradient(coeffs_ref, held_ref, grad_ref, slice(0, TE))
    total = before_ref[...] + dot(picked_ref[:TE, :], grad_ref[...], ((0,), (0,)))
    half = total.shape[1] // 2
    pieces_ref[:total.shape[0], :] = total[:, :half].astype(jnp.bfloat16)
    pieces_ref[total.shape[0]:, :] = total[:, half:].astype(jnp.bfloat16)


def left_kernel(left_ref, source_ref, relation_ref, *refs):
    out_ref = refs[-1]
    grads = jnp.concatenate([ref[...] for ref in refs[:-1]], axis=0)
    rows = left_ref.shape[0]
    for start in range(0, rows, TE):
        part = slice(start, start + TE)
        ids = lax.broadcasted_iota(jnp.int32, (TE, source_ref.shape[1]), 0) + start
        table = (ids == source_ref[...]).astype(jnp.float32).astype(jnp.bfloat16)
        summed = dot(table, grads, ((1,), (0,)))
        high = summed.astype(jnp.bfloat16)
        low = (summed - high.astype(jnp.float32)).astype(jnp.bfloat16)
        change = dot(high, relation_ref[...], ((1,), (1,))) + dot(low, relation_ref[...], ((1,), (1,)))
        out_ref[part, :] = (left_ref[part, :].astype(jnp.float32) - LR_EMBED * change).astype(jnp.bfloat16)


def sum_kernel(pieces_ref, copies_ref):
    lines = CODE_ROWS
    parts = [pieces_ref[k:k + lines, :].astype(jnp.float32) for k in range(0, pieces_ref.shape[0], lines)]
    total = functools.reduce(jnp.add, parts).astype(jnp.bfloat16)
    for k in range(0, copies_ref.shape[0], lines):
        copies_ref[k:k + lines, :] = total


def finish_kernel(gathered_ref, relation_ref, out_ref):
    rows, width = out_ref.shape
    half = width // 2
    for k in range(2):
        columns = slice(k * half, (k + 1) * half)
        total = gathered_ref[k * rows:(k + 1) * rows, :].astype(jnp.float32)
        out_ref[:, columns] = relation_ref[:, columns].astype(jnp.float32) - LR_RELATION * total


def copy_kernel(source_ref, out_ref):
    out_ref[...] = source_ref[...]


def call(kernel, outs, *args, scratch=()):
    spec = pl.BlockSpec(memory_space=VM)
    return pl.pallas_call(
        kernel,
        out_shape=outs,
        in_specs=[spec] * len(args),
        out_specs=jax.tree.map(lambda _: spec, outs),
        scratch_shapes=list(scratch),
        compiler_params=pltpu.CompilerParams(vmem_limit_bytes=16 << 20),
    )(*args)


def vmem(*shape):
    return VM(shape, jnp.bfloat16)


def local_meeting(meeting, queries, held, codes, relation, same, base):
    (edges, width), rows = queries.shape, held.shape[0]
    travel = vmem(TE + CODE_ROWS, width)
    outs = (vmem(rows, edges), vmem(edges, width), travel, travel)
    kernel = functools.partial(local_kernel, meeting)
    return call(kernel, outs, queries, held, codes, relation, same, base, scratch=[VM((rows, edges), jnp.float32)])


def first_half(picked, held, relation, before):
    rows, width = held.shape
    outs = (vmem(rows, TE), vmem(TE, width), vmem(TE, width), VM(before.shape, jnp.float32))
    return call(first_kernel, outs, picked, held, relation, before, scratch=[VM((rows, TE), jnp.float32)])


def held_half(picked, held, relation, coeffs, queries):
    rows, width = held.shape
    outs = (vmem(rows, width), vmem(rows, TE))
    scratch = [VM((rows, TE), jnp.float32)]
    return call(held_kernel, outs, picked, held, relation, coeffs, queries, scratch=scratch)


def last_half(picked, held, relation, before):
    rows, width = held.shape
    outs = (vmem(2 * width, width // 2), vmem(rows, TE), vmem(TE, width), vmem(TE, width))
    return call(last_kernel, outs, picked, held, relation, before, scratch=[VM((rows, TE), jnp.float32)])


def exchanged(pieces, axes, groups):
    rows, lanes = pieces.shape
    pieces = pieces.reshape(len(groups[0]), -1, lanes)
    return lax.all_to_all(pieces, axes, 0, 0, axis_index_groups=groups).reshape(rows, lanes)


def shared_sums(pieces):
    n_group, n_inner = lax.axis_size("group"), lax.axis_size("inner")
    depth = 8
    columns = range(n_inner // depth)
    planes = [[g * n_inner + x * depth + z for g in range(n_group) for x in columns] for z in range(depth)]
    lines = [[x * depth + z for z in range(depth)] for x in columns]
    rows, lanes = pieces.shape
    pieces = exchanged(pieces, AXES, planes)
    copies = call(sum_kernel, vmem(depth * CODE_ROWS, lanes), pieces)
    copies = call(sum_kernel, vmem(rows, lanes), exchanged(copies, "inner", lines))
    return exchanged(copies, AXES, planes)


def moved(value, mask):
    pairs = [(source, source ^ mask) for source in range(lax.axis_size("inner"))]
    return lax.ppermute(value, "inner", pairs)


def source_table(src_row, rows):
    return (src_row[:, None] == jnp.arange(rows, dtype=jnp.int32)[None, :]).astype(jnp.bfloat16)


def same_source(rows, columns):
    return (rows[:, None] == columns[None, :]).astype(jnp.bfloat16)


def picked_rows(left_block, table):
    return dot(table, left_block, ((1,), (0,))).astype(jnp.bfloat16)


def queries_of(picked, relation):
    return dot(picked, relation, ((1,), (0,))).astype(jnp.bfloat16)


def updated_holding(holding, *products):
    held_grad = functools.reduce(jnp.add, [dot(coeffs, queries, ((1,), (0,))) for coeffs, queries in products])
    return (holding.astype(jnp.float32) - (LR_EMBED * SCORE_SCALE) * held_grad).astype(jnp.bfloat16)


def query_gradient(coeffs, holding):
    return (dot(coeffs, holding, ((0,), (0,))) * SCORE_SCALE).astype(jnp.bfloat16)


def relation_gradient(picked, query_grad):
    return dot(picked, query_grad, ((0,), (0,)))


def updated_left(left_block, source, query_grads, relation, out):
    return call(left_kernel, out, left_block, source.reshape(1, -1), relation, *query_grads)


def coded(targets):
    meetings = targets.shape[0]
    lines = jnp.concatenate([targets // 32, targets % 32], axis=1).astype(jnp.bfloat16)
    lines = lines.reshape(meetings, -1, TE)
    lines = jnp.pad(lines, ((0, 0), (0, CODE_ROWS - lines.shape[1]), (0, 0)))
    return lines.reshape(meetings * CODE_ROWS, TE)


def shards(left_part, right_part, relation, src_index, dst_index, lengths):
    rows = left_part.shape[0]
    edges = src_index.shape[2]
    sources = src_index[0]

    held = moved(right_part, 1)
    slots = jnp.arange(edges, dtype=jnp.int32)
    targets = jnp.where(slots[None, :] < lengths[0][:, None], dst_index[0], -1)
    codes = coded(targets)
    tables = [source_table(sources[meeting], rows) for meeting in range(4)]
    picked0 = picked_rows(left_part, tables[0])
    queries0 = queries_of(picked0, relation)
    base = picked_rows(left_part, tables[1])
    same = same_source(sources[1], sources[0])
    coeffs, query_grad, first, second = local_meeting(0, queries0, held, codes, relation, same, base)

    first, second = moved(first, 2), moved(second, 2)
    held = updated_holding(held, (coeffs, queries0))
    left = updated_left(left_part, sources[0], [query_grad], relation, vmem(*left_part.shape))
    relation_grad = relation_gradient(picked0, query_grad)
    coeffs, queries, grad_a, relation_grad = first_half(first, held, relation, relation_grad)
    new_held, coeffs = held_half(second, held, relation, coeffs, queries)
    arriving = moved(new_held, 6)
    grad_b = query_gradient(coeffs, held)
    relation_grad = relation_grad + relation_gradient(second[:TE], grad_b)
    grads = [moved(grad_a, 2), moved(grad_b, 2)]
    left = updated_left(left, sources[1], grads, relation, vmem(*left.shape))

    held = arriving
    picked2 = picked_rows(left, tables[2])
    queries2 = queries_of(picked2, relation)
    base = picked_rows(left, tables[3])
    same = same_source(sources[3], sources[2])
    coeffs, query_grad, first, second = local_meeting(2, queries2, held, codes, relation, same, base)

    first, second = moved(first, 8), moved(second, 8)
    held = updated_holding(held, (coeffs, queries2))
    left = updated_left(left, sources[2], [query_grad], relation, vmem(*left.shape))
    relation_grad = relation_grad + relation_gradient(picked2, query_grad)
    coeffs_a, queries_a, grad_a, relation_grad = first_half(first, held, relation, relation_grad)
    pieces, coeffs_b, grad_b, queries_b = last_half(second, held, relation, relation_grad)
    sums = shared_sums(pieces)
    held = updated_holding(held, (coeffs_a, queries_a), (coeffs_b, queries_b))
    held = moved(held, 8)
    grads = [moved(grad_a, 8), moved(grad_b, 8)]
    last = jax.ShapeDtypeStruct(left.shape, left.dtype)
    left = updated_left(left, sources[3], grads, relation, last)
    held = call(copy_kernel, jax.ShapeDtypeStruct(held.shape, held.dtype), held)
    relation, held, left = lax.optimization_barrier((relation, held, left))
    relation_out = call(finish_kernel, jax.ShapeDtypeStruct(relation.shape, jnp.float32), sums, relation)
    return (left, held, relation_out)


def solution(mesh):
    in_specs = (
        P(AXES, None),
        P(AXES, None),
        P(),
        P(AXES, None, None),
        P(AXES, None, None),
        P(AXES, None),
    )
    out_specs = (P(AXES, None), P(AXES, None), P())
    return jax.shard_map(shards, mesh=mesh, in_specs=in_specs, out_specs=out_specs, check_vma=False)
```

```python
import functools
import jax
import jax.numpy as jnp
from jax import lax
from jax.experimental import pallas as pl
from jax.experimental.pallas import tpu as pltpu
from jax.sharding import PartitionSpec as P

SCORE_SCALE = 0.1875
LR_EMBED = 0.5
LR_RELATION = 0.02
EXP_SCALE = SCORE_SCALE * 1.4426950408889634
CODE_ROWS = 16
AXES = ("group", "inner")
VM = pltpu.VMEM
TE = 256


def dot(a, b, dims):
    return lax.dot_general(a, b, (dims, ((), ())), preferred_element_type=jnp.float32)


RC = 128


def scores_of(queries, held_ref, scores_ref, part):
    scores_ref[:, part] = dot(held_ref[...], queries[part], ((1,), (1,)))


def fill_coeffs(codes_ref, first, coeffs_ref, scores_ref, part):
    rows, edges = coeffs_ref.shape
    chunks = [slice(start, start + RC) for start in range(0, rows, RC)]
    fold = lambda value, op: functools.reduce(op, [value[k:k + 8] for k in range(0, value.shape[0], 8)])
    top = functools.reduce(jnp.maximum, [fold(scores_ref[c, part], jnp.maximum) for c in chunks])
    top = jnp.max(top, axis=0, keepdims=True)
    total = None
    for c in chunks:
        expos = jnp.exp2((scores_ref[c, part] - top) * EXP_SCALE)
        scores_ref[c, part] = expos
        folded = fold(expos, jnp.add)
        total = folded if total is None else total + folded
    high, low = first + part.start // TE, first + (edges + part.start) // TE
    target = codes_ref[high:high + 1, :].astype(jnp.float32) * 32.0 + codes_ref[low:low + 1, :].astype(jnp.float32)
    live = (target >= 0.0).astype(jnp.float32)
    weight = live / jnp.sum(total, axis=0, keepdims=True)
    ids = lax.broadcasted_iota(jnp.int32, (RC, TE), 0).astype(jnp.float32)
    for c in chunks:
        softmax_w = scores_ref[c, part] * weight
        coeffs = jnp.where(ids == target - float(c.start), softmax_w - 1.0, softmax_w)
        coeffs_ref[c, part] = coeffs.astype(jnp.bfloat16)


def parts_of(edges):
    return [slice(start, start + TE) for start in range(0, edges, TE)]


def fill_gradient(coeffs_ref, held_ref, grad_ref, part):
    grad = dot(coeffs_ref[:, part], held_ref[...], ((0,), (0,))) * SCORE_SCALE
    grad_ref[part, :] = grad.astype(jnp.bfloat16)


def meeting_body(queries, held_ref, codes_ref, first, coeffs_ref, scores_ref, then):
    parts = parts_of(coeffs_ref.shape[1])
    scores_of(queries, held_ref, scores_ref, parts[0])
    for k, part in enumerate(parts):
        if k + 1 < len(parts):
            scores_of(queries, held_ref, scores_ref, parts[k + 1])
        fill_coeffs(codes_ref, first, coeffs_ref, scores_ref, part)
        then(part)


def local_kernel(meeting, queries_ref, held_ref, codes_ref, relation_ref, same_ref, base_ref, coeffs_ref, grad_ref, next_ref, scores_ref):
    edges = queries_ref.shape[0]
    then = lambda part: fill_gradient(coeffs_ref, held_ref, grad_ref, part)
    meeting_body(queries_ref[...], held_ref, codes_ref, CODE_ROWS * meeting, coeffs_ref, scores_ref, then)
    summed = dot(same_ref[...], grad_ref[...], ((1,), (0,)))
    high = summed.astype(jnp.bfloat16)
    low = (summed - high.astype(jnp.float32)).astype(jnp.bfloat16)
    change = dot(high, relation_ref[...], ((1,), (1,))) + dot(low, relation_ref[...], ((1,), (1,)))
    next_ref[edges:, :] = codes_ref[CODE_ROWS * (meeting + 1):CODE_ROWS * (meeting + 2), :]
    next_ref[:edges, :] = (base_ref[...].astype(jnp.float32) - LR_EMBED * change).astype(jnp.bfloat16)


def coeffs_of(picked_ref, held_ref, relation_ref, coeffs_ref, scores_ref, then):
    edges = coeffs_ref.shape[1]
    queries = dot(picked_ref[:edges, :], relation_ref[...], ((1,), (0,))).astype(jnp.bfloat16)
    meeting_body(queries, held_ref, picked_ref, edges, coeffs_ref, scores_ref, then)
    return queries


def held_kernel(picked_ref, held_ref, relation_ref, new_ref, scores_ref, coeffs_ref):
    queries = coeffs_of(picked_ref, held_ref, relation_ref, coeffs_ref, scores_ref, lambda part: None)
    held_grad = dot(coeffs_ref[...], queries, ((1,), (0,)))
    new_ref[...] = (held_ref[...].astype(jnp.float32) - (LR_EMBED * SCORE_SCALE) * held_grad).astype(jnp.bfloat16)


def grad_kernel(picked_ref, held_ref, relation_ref, grad_ref, scores_ref, coeffs_ref):
    then = lambda part: fill_gradient(coeffs_ref, held_ref, grad_ref, part)
    coeffs_of(picked_ref, held_ref, relation_ref, coeffs_ref, scores_ref, then)


def last_kernel(picked_ref, held_ref, relation_ref, before_ref, pieces_ref, coeffs_ref, grad_ref, queries_ref, scores_ref):
    edges = coeffs_ref.shape[1]
    picked = picked_ref[:edges, :]
    queries = dot(picked, relation_ref[...], ((1,), (0,))).astype(jnp.bfloat16)
    queries_ref[...] = queries
    then = lambda part: fill_gradient(coeffs_ref, held_ref, grad_ref, part)
    meeting_body(queries, held_ref, picked_ref, edges, coeffs_ref, scores_ref, then)
    total = before_ref[...] + dot(picked, grad_ref[...], ((0,), (0,)))
    half = total.shape[1] // 2
    pieces_ref[:total.shape[0], :] = total[:, :half].astype(jnp.bfloat16)
    pieces_ref[total.shape[0]:, :] = total[:, half:].astype(jnp.bfloat16)


def left_kernel(left_ref, source_ref, grad_ref, relation_ref, out_ref):
    rows = left_ref.shape[0]
    for start in range(0, rows, TE):
        part = slice(start, start + TE)
        ids = lax.broadcasted_iota(jnp.int32, (TE, source_ref.shape[1]), 0) + start
        table = (ids == source_ref[...]).astype(jnp.float32).astype(jnp.bfloat16)
        summed = dot(table, grad_ref[...], ((1,), (0,)))
        high = summed.astype(jnp.bfloat16)
        low = (summed - high.astype(jnp.float32)).astype(jnp.bfloat16)
        change = dot(high, relation_ref[...], ((1,), (1,))) + dot(low, relation_ref[...], ((1,), (1,)))
        out_ref[part, :] = (left_ref[part, :].astype(jnp.float32) - LR_EMBED * change).astype(jnp.bfloat16)


def sum_kernel(pieces_ref, copies_ref):
    lines = CODE_ROWS
    parts = [pieces_ref[k:k + lines, :].astype(jnp.float32) for k in range(0, pieces_ref.shape[0], lines)]
    total = functools.reduce(jnp.add, parts).astype(jnp.bfloat16)
    for k in range(0, copies_ref.shape[0], lines):
        copies_ref[k:k + lines, :] = total


def finish_kernel(gathered_ref, relation_ref, out_ref):
    rows, width = out_ref.shape
    half = width // 2
    for k in range(2):
        columns = slice(k * half, (k + 1) * half)
        total = gathered_ref[k * rows:(k + 1) * rows, :].astype(jnp.float32)
        out_ref[:, columns] = relation_ref[:, columns].astype(jnp.float32) - LR_RELATION * total


def copy_kernel(source_ref, out_ref):
    out_ref[...] = source_ref[...]


def call(kernel, outs, *args, scratch=()):
    spec = pl.BlockSpec(memory_space=VM)
    return pl.pallas_call(
        kernel,
        out_shape=outs,
        in_specs=[spec] * len(args),
        out_specs=jax.tree.map(lambda _: spec, outs),
        scratch_shapes=list(scratch),
        compiler_params=pltpu.CompilerParams(vmem_limit_bytes=16 << 20),
    )(*args)


def vmem(*shape):
    return VM(shape, jnp.bfloat16)


def local_meeting(meeting, queries, held, codes, relation, same, base):
    (edges, width), rows = queries.shape, held.shape[0]
    outs = (vmem(rows, edges), vmem(edges, width), vmem(edges + CODE_ROWS, width))
    scratch = [VM((rows, edges), jnp.float32)]
    return call(functools.partial(local_kernel, meeting), outs, queries, held, codes, relation, same, base, scratch=scratch)


def row_kernel(kernel, out, picked, held, relation):
    rows, edges = held.shape[0], picked.shape[0] - CODE_ROWS
    scratch = [VM((rows, edges), jnp.float32), vmem(rows, edges)]
    return call(kernel, out, picked, held, relation, scratch=scratch)


def replayed(picked, held, relation):
    return row_kernel(held_kernel, vmem(*held.shape), picked, held, relation)


def gradient_at_host(picked, held, relation):
    out = vmem(picked.shape[0] - CODE_ROWS, held.shape[1])
    return row_kernel(grad_kernel, out, picked, held, relation)


def last_meeting(picked, held, relation, before, edges):
    rows, width = held.shape
    outs = (vmem(2 * width, width // 2), vmem(rows, edges), vmem(edges, width), vmem(edges, width))
    scratch = [VM((rows, edges), jnp.float32)]
    return call(last_kernel, outs, picked, held, relation, before, scratch=scratch)


def exchanged(pieces, axes, groups):
    rows, lanes = pieces.shape
    pieces = pieces.reshape(len(groups[0]), -1, lanes)
    return lax.all_to_all(pieces, axes, 0, 0, axis_index_groups=groups).reshape(rows, lanes)


def shared_sums(pieces):
    n_group, n_inner = lax.axis_size("group"), lax.axis_size("inner")
    depth = 8
    columns = range(n_inner // depth)
    planes = [[g * n_inner + x * depth + z for g in range(n_group) for x in columns] for z in range(depth)]
    lines = [[x * depth + z for z in range(depth)] for x in columns]
    rows, lanes = pieces.shape
    pieces = exchanged(pieces, AXES, planes)
    copies = call(sum_kernel, vmem(depth * CODE_ROWS, lanes), pieces)
    copies = call(sum_kernel, vmem(rows, lanes), exchanged(copies, "inner", lines))
    return exchanged(copies, AXES, planes)


def moved(value, mask):
    pairs = [(source, source ^ mask) for source in range(lax.axis_size("inner"))]
    return lax.ppermute(value, "inner", pairs)


def source_table(src_row, rows):
    return (src_row[:, None] == jnp.arange(rows, dtype=jnp.int32)[None, :]).astype(jnp.bfloat16)


def same_source(rows, columns):
    return (rows[:, None] == columns[None, :]).astype(jnp.bfloat16)


def picked_rows(left_block, table):
    return dot(table, left_block, ((1,), (0,))).astype(jnp.bfloat16)


def queries_of(picked, relation):
    return dot(picked, relation, ((1,), (0,))).astype(jnp.bfloat16)


def updated_holding(holding, coeffs, queries):
    held_grad = dot(coeffs, queries, ((1,), (0,)))
    return (holding.astype(jnp.float32) - (LR_EMBED * SCORE_SCALE) * held_grad).astype(jnp.bfloat16)


def relation_gradient(picked, query_grad):
    return dot(picked, query_grad, ((0,), (0,)))


def updated_left(left_block, source, query_grad, relation, out):
    return call(left_kernel, out, left_block, source.reshape(1, -1), query_grad, relation)


def coded(targets):
    meetings = targets.shape[0]
    lines = jnp.concatenate([targets // 32, targets % 32], axis=1).astype(jnp.bfloat16)
    lines = lines.reshape(meetings, -1, TE)
    lines = jnp.pad(lines, ((0, 0), (0, CODE_ROWS - lines.shape[1]), (0, 0)))
    return lines.reshape(meetings * CODE_ROWS, TE)


def shards(left_part, right_part, relation, src_index, dst_index, lengths):
    rows = left_part.shape[0]
    edges = src_index.shape[2]
    sources = src_index[0]

    held = moved(right_part, 1)
    far = moved(right_part, 7)
    slots = jnp.arange(edges, dtype=jnp.int32)
    targets = jnp.where(slots[None, :] < lengths[0][:, None], dst_index[0], -1)
    codes = coded(targets)
    tables = [source_table(sources[meeting], rows) for meeting in range(4)]
    picked0 = picked_rows(left_part, tables[0])
    rows0 = moved(jnp.concatenate([picked0, codes[:CODE_ROWS]], axis=0), 6)
    queries0 = queries_of(picked0, relation)
    base = picked_rows(left_part, tables[1])
    same = same_source(sources[1], sources[0])
    coeffs, query_grad, picked1 = local_meeting(0, queries0, held, codes, relation, same, base)

    rows1 = moved(picked1, 2)
    held = updated_holding(held, coeffs, queries0)
    left = updated_left(left_part, sources[0], query_grad, relation, vmem(*left_part.shape))
    relation_grad = relation_gradient(picked0, query_grad)
    query_grad = gradient_at_host(rows1, held, relation)
    back1 = moved(query_grad, 2)
    onward = moved(rows1, 6)
    relation_grad = relation_grad + relation_gradient(rows1[:edges], query_grad)
    left = updated_left(left, sources[1], back1, relation, vmem(*left.shape))

    held = replayed(onward, replayed(rows0, far, relation), relation)
    picked2 = picked_rows(left, tables[2])
    queries2 = queries_of(picked2, relation)
    base = picked_rows(left, tables[3])
    same = same_source(sources[3], sources[2])
    coeffs, query_grad, picked3 = local_meeting(2, queries2, held, codes, relation, same, base)

    rows3 = moved(picked3, 8)
    held = updated_holding(held, coeffs, queries2)
    left = updated_left(left, sources[2], query_grad, relation, vmem(*left.shape))
    relation_grad = relation_grad + relation_gradient(picked2, query_grad)
    pieces, coeffs, query_grad, queries3 = last_meeting(rows3, held, relation, relation_grad, edges)
    sums = shared_sums(pieces)
    held = updated_holding(held, coeffs, queries3)
    held = moved(held, 8)
    last = jax.ShapeDtypeStruct(left.shape, left.dtype)
    left = updated_left(left, sources[3], moved(query_grad, 8), relation, last)
    held = call(copy_kernel, jax.ShapeDtypeStruct(held.shape, held.dtype), held)
    relation, held, left = lax.optimization_barrier((relation, held, left))
    relation_out = call(finish_kernel, jax.ShapeDtypeStruct(relation.shape, jnp.float32), sums, relation)
    return (left, held, relation_out)


def solution(mesh):
    in_specs = (
        P(AXES, None),
        P(AXES, None),
        P(),
        P(AXES, None, None),
        P(AXES, None, None),
        P(AXES, None),
    )
    out_specs = (P(AXES, None), P(AXES, None), P())
    return jax.shard_map(shards, mesh=mesh, in_specs=in_specs, out_specs=out_specs, check_vma=False)
```

```python
import functools
import jax
import jax.numpy as jnp
from jax import lax
from jax.experimental import pallas as pl
from jax.experimental.pallas import tpu as pltpu
from jax.sharding import PartitionSpec as P

SCORE_SCALE = 0.1875
LR_EMBED = 0.5
LR_RELATION = 0.02
EXP_SCALE = SCORE_SCALE * 1.4426950408889634
CODE_ROWS = 16
AXES = ("group", "inner")
VM = pltpu.VMEM
TE = 256


def dot(a, b, dims):
    return lax.dot_general(a, b, (dims, ((), ())), preferred_element_type=jnp.float32)


RC = 128


def scores_of(queries, held_ref, scores_ref, part):
    scores_ref[:, part] = dot(held_ref[...], queries[part], ((1,), (1,)))


def fill_coeffs(codes_ref, first, coeffs_ref, scores_ref, part):
    rows, edges = coeffs_ref.shape
    chunks = [slice(start, start + RC) for start in range(0, rows, RC)]
    fold = lambda value, op: functools.reduce(op, [value[k:k + 8] for k in range(0, value.shape[0], 8)])
    top = functools.reduce(jnp.maximum, [fold(scores_ref[c, part], jnp.maximum) for c in chunks])
    top = jnp.max(top, axis=0, keepdims=True)
    total = None
    for c in chunks:
        expos = jnp.exp2((scores_ref[c, part] - top) * EXP_SCALE)
        scores_ref[c, part] = expos
        folded = fold(expos, jnp.add)
        total = folded if total is None else total + folded
    high, low = first + part.start // TE, first + (edges + part.start) // TE
    target = codes_ref[high:high + 1, :].astype(jnp.float32) * 32.0 + codes_ref[low:low + 1, :].astype(jnp.float32)
    live = (target >= 0.0).astype(jnp.float32)
    weight = live / jnp.sum(total, axis=0, keepdims=True)
    ids = lax.broadcasted_iota(jnp.int32, (RC, TE), 0).astype(jnp.float32)
    for c in chunks:
        softmax_w = scores_ref[c, part] * weight
        coeffs = jnp.where(ids == target - float(c.start), softmax_w - 1.0, softmax_w)
        coeffs_ref[c, part] = coeffs.astype(jnp.bfloat16)


def parts_of(edges):
    return [slice(start, start + TE) for start in range(0, edges, TE)]


def fill_gradient(coeffs_ref, held_ref, grad_ref, part):
    grad = dot(coeffs_ref[:, part], held_ref[...], ((0,), (0,))) * SCORE_SCALE
    grad_ref[part, :] = grad.astype(jnp.bfloat16)


def meeting_body(queries, held_ref, codes_ref, first, coeffs_ref, scores_ref, then):
    parts = parts_of(coeffs_ref.shape[1])
    scores_of(queries, held_ref, scores_ref, parts[0])
    for k, part in enumerate(parts):
        if k + 1 < len(parts):
            scores_of(queries, held_ref, scores_ref, parts[k + 1])
        fill_coeffs(codes_ref, first, coeffs_ref, scores_ref, part)
        then(part)


def local_kernel(meeting, queries_ref, held_ref, codes_ref, relation_ref, same_ref, base_ref, coeffs_ref, grad_ref, next_ref, scores_ref):
    edges = queries_ref.shape[0]
    then = lambda part: fill_gradient(coeffs_ref, held_ref, grad_ref, part)
    meeting_body(queries_ref[...], held_ref, codes_ref, CODE_ROWS * meeting, coeffs_ref, scores_ref, then)
    summed = dot(same_ref[...], grad_ref[...], ((1,), (0,)))
    high = summed.astype(jnp.bfloat16)
    low = (summed - high.astype(jnp.float32)).astype(jnp.bfloat16)
    change = dot(high, relation_ref[...], ((1,), (1,))) + dot(low, relation_ref[...], ((1,), (1,)))
    next_ref[edges:, :] = codes_ref[CODE_ROWS * (meeting + 1):CODE_ROWS * (meeting + 2), :]
    next_ref[:edges, :] = (base_ref[...].astype(jnp.float32) - LR_EMBED * change).astype(jnp.bfloat16)


def coeffs_of(picked_ref, held_ref, relation_ref, coeffs_ref, scores_ref, then):
    edges = coeffs_ref.shape[1]
    queries = dot(picked_ref[:edges, :], relation_ref[...], ((1,), (0,))).astype(jnp.bfloat16)
    meeting_body(queries, held_ref, picked_ref, edges, coeffs_ref, scores_ref, then)
    return queries


def held_kernel(picked_ref, held_ref, relation_ref, new_ref, scores_ref, coeffs_ref):
    queries = coeffs_of(picked_ref, held_ref, relation_ref, coeffs_ref, scores_ref, lambda part: None)
    held_grad = dot(coeffs_ref[...], queries, ((1,), (0,)))
    new_ref[...] = (held_ref[...].astype(jnp.float32) - (LR_EMBED * SCORE_SCALE) * held_grad).astype(jnp.bfloat16)


def host_kernel(picked_ref, held_ref, relation_ref, new_ref, grad_ref, scores_ref, coeffs_ref):
    then = lambda part: fill_gradient(coeffs_ref, held_ref, grad_ref, part)
    queries = coeffs_of(picked_ref, held_ref, relation_ref, coeffs_ref, scores_ref, then)
    held_grad = dot(coeffs_ref[...], queries, ((1,), (0,)))
    new_ref[...] = (held_ref[...].astype(jnp.float32) - (LR_EMBED * SCORE_SCALE) * held_grad).astype(jnp.bfloat16)


def choice_kernel(flag_ref, picked_ref, held_ref, relation_ref, arrived_ref, new_ref, scores_ref, coeffs_ref):
    @pl.when(flag_ref[0] == 1)
    def _():
        held_kernel(picked_ref, held_ref, relation_ref, new_ref, scores_ref, coeffs_ref)

    @pl.when(flag_ref[0] == 0)
    def _():
        new_ref[...] = arrived_ref[...]


def last_kernel(picked_ref, held_ref, relation_ref, before_ref, pieces_ref, coeffs_ref, grad_ref, queries_ref, scores_ref):
    edges = coeffs_ref.shape[1]
    picked = picked_ref[:edges, :]
    queries = dot(picked, relation_ref[...], ((1,), (0,))).astype(jnp.bfloat16)
    queries_ref[...] = queries
    then = lambda part: fill_gradient(coeffs_ref, held_ref, grad_ref, part)
    meeting_body(queries, held_ref, picked_ref, edges, coeffs_ref, scores_ref, then)
    total = before_ref[...] + dot(picked, grad_ref[...], ((0,), (0,)))
    half = total.shape[1] // 2
    pieces_ref[:total.shape[0], :] = total[:, :half].astype(jnp.bfloat16)
    pieces_ref[total.shape[0]:, :] = total[:, half:].astype(jnp.bfloat16)


def left_kernel(left_ref, source_ref, grad_ref, relation_ref, out_ref):
    rows = left_ref.shape[0]
    for start in range(0, rows, TE):
        part = slice(start, start + TE)
        ids = lax.broadcasted_iota(jnp.int32, (TE, source_ref.shape[1]), 0) + start
        table = (ids == source_ref[...]).astype(jnp.float32).astype(jnp.bfloat16)
        summed = dot(table, grad_ref[...], ((1,), (0,)))
        high = summed.astype(jnp.bfloat16)
        low = (summed - high.astype(jnp.float32)).astype(jnp.bfloat16)
        change = dot(high, relation_ref[...], ((1,), (1,))) + dot(low, relation_ref[...], ((1,), (1,)))
        out_ref[part, :] = (left_ref[part, :].astype(jnp.float32) - LR_EMBED * change).astype(jnp.bfloat16)


def sum_kernel(pieces_ref, copies_ref):
    lines = CODE_ROWS
    parts = [pieces_ref[k:k + lines, :].astype(jnp.float32) for k in range(0, pieces_ref.shape[0], lines)]
    total = functools.reduce(jnp.add, parts).astype(jnp.bfloat16)
    for k in range(0, copies_ref.shape[0], lines):
        copies_ref[k:k + lines, :] = total


def finish_kernel(gathered_ref, relation_ref, out_ref):
    rows, width = out_ref.shape
    half = width // 2
    for k in range(2):
        columns = slice(k * half, (k + 1) * half)
        total = gathered_ref[k * rows:(k + 1) * rows, :].astype(jnp.float32)
        out_ref[:, columns] = relation_ref[:, columns].astype(jnp.float32) - LR_RELATION * total


def copy_kernel(source_ref, out_ref):
    out_ref[...] = source_ref[...]


def call(kernel, outs, *args, scratch=()):
    spec = pl.BlockSpec(memory_space=VM)
    flags = pl.BlockSpec(memory_space=pltpu.SMEM)
    return pl.pallas_call(
        kernel,
        out_shape=outs,
        in_specs=[flags if arg.ndim == 1 else spec for arg in args],
        out_specs=jax.tree.map(lambda _: spec, outs),
        scratch_shapes=list(scratch),
        compiler_params=pltpu.CompilerParams(vmem_limit_bytes=16 << 20),
    )(*args)


def vmem(*shape):
    return VM(shape, jnp.bfloat16)


def local_meeting(meeting, queries, held, codes, relation, same, base):
    (edges, width), rows = queries.shape, held.shape[0]
    outs = (vmem(rows, edges), vmem(edges, width), vmem(edges + CODE_ROWS, width))
    scratch = [VM((rows, edges), jnp.float32)]
    return call(functools.partial(local_kernel, meeting), outs, queries, held, codes, relation, same, base, scratch=scratch)


def row_kernel(kernel, out, picked, held, relation, flag=(), arrived=()):
    rows, edges = held.shape[0], picked.shape[0] - CODE_ROWS
    scratch = [VM((rows, edges), jnp.float32), vmem(rows, edges)]
    return call(kernel, out, *flag, picked, held, relation, *arrived, scratch=scratch)


def host_meeting(picked, held, relation):
    outs = (vmem(*held.shape), vmem(picked.shape[0] - CODE_ROWS, held.shape[1]))
    return row_kernel(host_kernel, outs, picked, held, relation)


def last_meeting(picked, held, relation, before, edges):
    rows, width = held.shape
    outs = (vmem(2 * width, width // 2), vmem(rows, edges), vmem(edges, width), vmem(edges, width))
    scratch = [VM((rows, edges), jnp.float32)]
    return call(last_kernel, outs, picked, held, relation, before, scratch=scratch)


def exchanged(pieces, axes, groups):
    rows, lanes = pieces.shape
    pieces = pieces.reshape(len(groups[0]), -1, lanes)
    return lax.all_to_all(pieces, axes, 0, 0, axis_index_groups=groups).reshape(rows, lanes)


def shared_sums(pieces):
    n_group, n_inner = lax.axis_size("group"), lax.axis_size("inner")
    depth = 8
    columns = range(n_inner // depth)
    planes = [[g * n_inner + x * depth + z for g in range(n_group) for x in columns] for z in range(depth)]
    lines = [[x * depth + z for z in range(depth)] for x in columns]
    rows, lanes = pieces.shape
    pieces = exchanged(pieces, AXES, planes)
    copies = call(sum_kernel, vmem(depth * CODE_ROWS, lanes), pieces)
    copies = call(sum_kernel, vmem(rows, lanes), exchanged(copies, "inner", lines))
    return exchanged(copies, AXES, planes)


def direct(place):
    return ((place ^ (place >> 1)) & 1) == 0


def moved(value, mask, senders=lambda place: True):
    places = range(lax.axis_size("inner"))
    pairs = [(source, source ^ mask) for source in places if senders(source)]
    return lax.ppermute(value, "inner", pairs)


def source_table(src_row, rows):
    return (src_row[:, None] == jnp.arange(rows, dtype=jnp.int32)[None, :]).astype(jnp.bfloat16)


def same_source(rows, columns):
    return (rows[:, None] == columns[None, :]).astype(jnp.bfloat16)


def picked_rows(left_block, table):
    return dot(table, left_block, ((1,), (0,))).astype(jnp.bfloat16)


def queries_of(picked, relation):
    return dot(picked, relation, ((1,), (0,))).astype(jnp.bfloat16)


def updated_holding(holding, coeffs, queries):
    held_grad = dot(coeffs, queries, ((1,), (0,)))
    return (holding.astype(jnp.float32) - (LR_EMBED * SCORE_SCALE) * held_grad).astype(jnp.bfloat16)


def relation_gradient(picked, query_grad):
    return dot(picked, query_grad, ((0,), (0,)))


def updated_left(left_block, source, query_grad, relation, out):
    return call(left_kernel, out, left_block, source.reshape(1, -1), query_grad, relation)


def coded(targets):
    meetings = targets.shape[0]
    lines = jnp.concatenate([targets // 32, targets % 32], axis=1).astype(jnp.bfloat16)
    lines = lines.reshape(meetings, -1, TE)
    lines = jnp.pad(lines, ((0, 0), (0, CODE_ROWS - lines.shape[1]), (0, 0)))
    return lines.reshape(meetings * CODE_ROWS, TE)


def shards(left_part, right_part, relation, src_index, dst_index, lengths):
    rows = left_part.shape[0]
    edges = src_index.shape[2]
    sources = src_index[0]

    held = moved(right_part, 1)
    far = moved(right_part, 7, direct)
    slots = jnp.arange(edges, dtype=jnp.int32)
    targets = jnp.where(slots[None, :] < lengths[0][:, None], dst_index[0], -1)
    codes = coded(targets)
    tables = [source_table(sources[meeting], rows) for meeting in range(4)]
    picked0 = picked_rows(left_part, tables[0])
    rows0 = moved(jnp.concatenate([picked0, codes[:CODE_ROWS]], axis=0), 6, lambda place: not direct(place))
    queries0 = queries_of(picked0, relation)
    base = picked_rows(left_part, tables[1])
    same = same_source(sources[1], sources[0])
    coeffs, query_grad, picked1 = local_meeting(0, queries0, held, codes, relation, same, base)

    rows1 = moved(picked1, 2)
    held = updated_holding(held, coeffs, queries0)
    left = updated_left(left_part, sources[0], query_grad, relation, vmem(*left_part.shape))
    relation_grad = relation_gradient(picked0, query_grad)
    onward = moved(rows1, 6, lambda place: not direct(place))
    new_held, query_grad = host_meeting(rows1, held, relation)
    back1 = moved(query_grad, 2)
    arriving = moved(new_held, 6, direct)
    relation_grad = relation_grad + relation_gradient(rows1[:edges], query_grad)
    left = updated_left(left, sources[1], back1, relation, vmem(*left.shape))

    flag = direct(lax.axis_index("inner")).astype(jnp.int32).reshape(1)
    far = row_kernel(held_kernel, vmem(*far.shape), rows0, far, relation)
    held = row_kernel(choice_kernel, vmem(*far.shape), onward, far, relation, [flag], [arriving])
    picked2 = picked_rows(left, tables[2])
    queries2 = queries_of(picked2, relation)
    base = picked_rows(left, tables[3])
    same = same_source(sources[3], sources[2])
    coeffs, query_grad, picked3 = local_meeting(2, queries2, held, codes, relation, same, base)

    rows3 = moved(picked3, 8)
    held = updated_holding(held, coeffs, queries2)
    left = updated_left(left, sources[2], query_grad, relation, vmem(*left.shape))
    relation_grad = relation_grad + relation_gradient(picked2, query_grad)
    pieces, coeffs, query_grad, queries3 = last_meeting(rows3, held, relation, relation_grad, edges)
    sums = shared_sums(pieces)
    held = updated_holding(held, coeffs, queries3)
    held = moved(held, 8)
    last = jax.ShapeDtypeStruct(left.shape, left.dtype)
    left = updated_left(left, sources[3], moved(query_grad, 8), relation, last)
    held = call(copy_kernel, jax.ShapeDtypeStruct(held.shape, held.dtype), held)
    relation, held, left = lax.optimization_barrier((relation, held, left))
    relation_out = call(finish_kernel, jax.ShapeDtypeStruct(relation.shape, jnp.float32), sums, relation)
    return (left, held, relation_out)


def solution(mesh):
    in_specs = (
        P(AXES, None),
        P(AXES, None),
        P(),
        P(AXES, None, None),
        P(AXES, None, None),
        P(AXES, None),
    )
    out_specs = (P(AXES, None), P(AXES, None), P())
    return jax.shard_map(shards, mesh=mesh, in_specs=in_specs, out_specs=out_specs, check_vma=False)
```

```python
import functools
import jax
import jax.numpy as jnp
from jax import lax
from jax.experimental import pallas as pl
from jax.experimental.pallas import tpu as pltpu
from jax.sharding import PartitionSpec as P

SCORE_SCALE = 0.1875
LR_EMBED = 0.5
LR_RELATION = 0.02
EXP_SCALE = SCORE_SCALE * 1.4426950408889634
CODE_ROWS = 16
AXES = ("group", "inner")
VM = pltpu.VMEM
TE = 256


def dot(a, b, dims):
    return lax.dot_general(a, b, (dims, ((), ())), preferred_element_type=jnp.float32)


RC = 128


def scores_of(queries, held_ref, scores_ref, part):
    scores_ref[:, part] = dot(held_ref[...], queries[part], ((1,), (1,)))


def fill_coeffs(codes_ref, first, coeffs_ref, scores_ref, part):
    rows, edges = coeffs_ref.shape
    chunks = [slice(start, start + RC) for start in range(0, rows, RC)]
    fold = lambda value, op: functools.reduce(op, [value[k:k + 8] for k in range(0, value.shape[0], 8)])
    top = functools.reduce(jnp.maximum, [fold(scores_ref[c, part], jnp.maximum) for c in chunks])
    top = jnp.max(top, axis=0, keepdims=True)
    total = None
    for c in chunks:
        expos = jnp.exp2((scores_ref[c, part] - top) * EXP_SCALE)
        scores_ref[c, part] = expos
        folded = fold(expos, jnp.add)
        total = folded if total is None else total + folded
    high, low = first + part.start // TE, first + (edges + part.start) // TE
    target = codes_ref[high:high + 1, :].astype(jnp.float32) * 32.0 + codes_ref[low:low + 1, :].astype(jnp.float32)
    live = (target >= 0.0).astype(jnp.float32)
    weight = live / jnp.sum(total, axis=0, keepdims=True)
    ids = lax.broadcasted_iota(jnp.int32, (RC, TE), 0).astype(jnp.float32)
    for c in chunks:
        softmax_w = scores_ref[c, part] * weight
        coeffs = jnp.where(ids == target - float(c.start), softmax_w - 1.0, softmax_w)
        coeffs_ref[c, part] = coeffs.astype(jnp.bfloat16)


def parts_of(edges):
    return [slice(start, start + TE) for start in range(0, edges, TE)]


def fill_gradient(coeffs_ref, held_ref, grad_ref, part):
    grad = dot(coeffs_ref[:, part], held_ref[...], ((0,), (0,))) * SCORE_SCALE
    grad_ref[part, :] = grad.astype(jnp.bfloat16)


def meeting_body(queries, held_ref, codes_ref, first, coeffs_ref, scores_ref, then):
    parts = parts_of(coeffs_ref.shape[1])
    scores_of(queries, held_ref, scores_ref, parts[0])
    for k, part in enumerate(parts):
        if k + 1 < len(parts):
            scores_of(queries, held_ref, scores_ref, parts[k + 1])
        fill_coeffs(codes_ref, first, coeffs_ref, scores_ref, part)
        then(part)


def local_kernel(meeting, queries_ref, held_ref, codes_ref, relation_ref, same_ref, base_ref, coeffs_ref, grad_ref, next_ref, scores_ref):
    edges = queries_ref.shape[0]
    then = lambda part: fill_gradient(coeffs_ref, held_ref, grad_ref, part)
    meeting_body(queries_ref[...], held_ref, codes_ref, CODE_ROWS * meeting, coeffs_ref, scores_ref, then)
    summed = dot(same_ref[...], grad_ref[...], ((1,), (0,)))
    high = summed.astype(jnp.bfloat16)
    low = (summed - high.astype(jnp.float32)).astype(jnp.bfloat16)
    change = dot(high, relation_ref[...], ((1,), (1,))) + dot(low, relation_ref[...], ((1,), (1,)))
    next_ref[edges:, :] = codes_ref[CODE_ROWS * (meeting + 1):CODE_ROWS * (meeting + 2), :]
    next_ref[:edges, :] = (base_ref[...].astype(jnp.float32) - LR_EMBED * change).astype(jnp.bfloat16)


def coeffs_of(picked_ref, held_ref, relation_ref, coeffs_ref, scores_ref, then):
    edges = coeffs_ref.shape[1]
    queries = dot(picked_ref[:edges, :], relation_ref[...], ((1,), (0,))).astype(jnp.bfloat16)
    meeting_body(queries, held_ref, picked_ref, edges, coeffs_ref, scores_ref, then)
    return queries


def held_kernel(picked_ref, held_ref, relation_ref, new_ref, scores_ref, coeffs_ref):
    queries = coeffs_of(picked_ref, held_ref, relation_ref, coeffs_ref, scores_ref, lambda part: None)
    held_grad = dot(coeffs_ref[...], queries, ((1,), (0,)))
    new_ref[...] = (held_ref[...].astype(jnp.float32) - (LR_EMBED * SCORE_SCALE) * held_grad).astype(jnp.bfloat16)


def grad_kernel(picked_ref, held_ref, relation_ref, grad_ref, scores_ref, coeffs_ref):
    then = lambda part: fill_gradient(coeffs_ref, held_ref, grad_ref, part)
    coeffs_of(picked_ref, held_ref, relation_ref, coeffs_ref, scores_ref, then)


def choice_kernel(flag_ref, picked_ref, held_ref, relation_ref, arrived_ref, new_ref, scores_ref, coeffs_ref):
    @pl.when(flag_ref[0] == 1)
    def _():
        held_kernel(picked_ref, held_ref, relation_ref, new_ref, scores_ref, coeffs_ref)

    @pl.when(flag_ref[0] == 0)
    def _():
        new_ref[...] = arrived_ref[...]


def last_kernel(picked_ref, held_ref, relation_ref, before_ref, pieces_ref, coeffs_ref, grad_ref, queries_ref, scores_ref):
    edges = coeffs_ref.shape[1]
    picked = picked_ref[:edges, :]
    queries = dot(picked, relation_ref[...], ((1,), (0,))).astype(jnp.bfloat16)
    queries_ref[...] = queries
    then = lambda part: fill_gradient(coeffs_ref, held_ref, grad_ref, part)
    meeting_body(queries, held_ref, picked_ref, edges, coeffs_ref, scores_ref, then)
    total = before_ref[...] + dot(picked, grad_ref[...], ((0,), (0,)))
    half = total.shape[1] // 2
    pieces_ref[:total.shape[0], :] = total[:, :half].astype(jnp.bfloat16)
    pieces_ref[total.shape[0]:, :] = total[:, half:].astype(jnp.bfloat16)


def left_kernel(left_ref, source_ref, grad_ref, relation_ref, out_ref):
    rows = left_ref.shape[0]
    for start in range(0, rows, TE):
        part = slice(start, start + TE)
        ids = lax.broadcasted_iota(jnp.int32, (TE, source_ref.shape[1]), 0) + start
        table = (ids == source_ref[...]).astype(jnp.float32).astype(jnp.bfloat16)
        summed = dot(table, grad_ref[...], ((1,), (0,)))
        high = summed.astype(jnp.bfloat16)
        low = (summed - high.astype(jnp.float32)).astype(jnp.bfloat16)
        change = dot(high, relation_ref[...], ((1,), (1,))) + dot(low, relation_ref[...], ((1,), (1,)))
        out_ref[part, :] = (left_ref[part, :].astype(jnp.float32) - LR_EMBED * change).astype(jnp.bfloat16)


def sum_kernel(pieces_ref, copies_ref):
    lines = CODE_ROWS
    parts = [pieces_ref[k:k + lines, :].astype(jnp.float32) for k in range(0, pieces_ref.shape[0], lines)]
    total = functools.reduce(jnp.add, parts).astype(jnp.bfloat16)
    for k in range(0, copies_ref.shape[0], lines):
        copies_ref[k:k + lines, :] = total


def finish_kernel(gathered_ref, relation_ref, out_ref):
    rows, width = out_ref.shape
    half = width // 2
    for k in range(2):
        columns = slice(k * half, (k + 1) * half)
        total = gathered_ref[k * rows:(k + 1) * rows, :].astype(jnp.float32)
        out_ref[:, columns] = relation_ref[:, columns].astype(jnp.float32) - LR_RELATION * total


def copy_kernel(source_ref, out_ref):
    out_ref[...] = source_ref[...]


def call(kernel, outs, *args, scratch=()):
    spec = pl.BlockSpec(memory_space=VM)
    flags = pl.BlockSpec(memory_space=pltpu.SMEM)
    return pl.pallas_call(
        kernel,
        out_shape=outs,
        in_specs=[flags if arg.ndim == 1 else spec for arg in args],
        out_specs=jax.tree.map(lambda _: spec, outs),
        scratch_shapes=list(scratch),
        compiler_params=pltpu.CompilerParams(vmem_limit_bytes=16 << 20),
    )(*args)


def vmem(*shape):
    return VM(shape, jnp.bfloat16)


def local_meeting(meeting, queries, held, codes, relation, same, base):
    (edges, width), rows = queries.shape, held.shape[0]
    outs = (vmem(rows, edges), vmem(edges, width), vmem(edges + CODE_ROWS, width))
    scratch = [VM((rows, edges), jnp.float32)]
    return call(functools.partial(local_kernel, meeting), outs, queries, held, codes, relation, same, base, scratch=scratch)


def row_kernel(kernel, out, picked, held, relation, flag=(), arrived=()):
    rows, edges = held.shape[0], picked.shape[0] - CODE_ROWS
    scratch = [VM((rows, edges), jnp.float32), vmem(rows, edges)]
    return call(kernel, out, *flag, picked, held, relation, *arrived, scratch=scratch)


def last_meeting(picked, held, relation, before, edges):
    rows, width = held.shape
    outs = (vmem(2 * width, width // 2), vmem(rows, edges), vmem(edges, width), vmem(edges, width))
    scratch = [VM((rows, edges), jnp.float32)]
    return call(last_kernel, outs, picked, held, relation, before, scratch=scratch)


def exchanged(pieces, axes, groups):
    rows, lanes = pieces.shape
    pieces = pieces.reshape(len(groups[0]), -1, lanes)
    return lax.all_to_all(pieces, axes, 0, 0, axis_index_groups=groups).reshape(rows, lanes)


def shared_sums(pieces):
    n_group, n_inner = lax.axis_size("group"), lax.axis_size("inner")
    depth = 8
    columns = range(n_inner // depth)
    planes = [[g * n_inner + x * depth + z for g in range(n_group) for x in columns] for z in range(depth)]
    lines = [[x * depth + z for z in range(depth)] for x in columns]
    rows, lanes = pieces.shape
    pieces = exchanged(pieces, AXES, planes)
    copies = call(sum_kernel, vmem(depth * CODE_ROWS, lanes), pieces)
    copies = call(sum_kernel, vmem(rows, lanes), exchanged(copies, "inner", lines))
    return exchanged(copies, AXES, planes)


def direct(place):
    return ((place ^ (place >> 1)) & 1) == 0


def moved(value, mask, senders=lambda place: True):
    places = range(lax.axis_size("inner"))
    pairs = [(source, source ^ mask) for source in places if senders(source)]
    return lax.ppermute(value, "inner", pairs)


def source_table(src_row, rows):
    return (src_row[:, None] == jnp.arange(rows, dtype=jnp.int32)[None, :]).astype(jnp.bfloat16)


def same_source(rows, columns):
    return (rows[:, None] == columns[None, :]).astype(jnp.bfloat16)


def picked_rows(left_block, table):
    return dot(table, left_block, ((1,), (0,))).astype(jnp.bfloat16)


def queries_of(picked, relation):
    return dot(picked, relation, ((1,), (0,))).astype(jnp.bfloat16)


def updated_holding(holding, coeffs, queries):
    held_grad = dot(coeffs, queries, ((1,), (0,)))
    return (holding.astype(jnp.float32) - (LR_EMBED * SCORE_SCALE) * held_grad).astype(jnp.bfloat16)


def relation_gradient(picked, query_grad):
    return dot(picked, query_grad, ((0,), (0,)))


def updated_left(left_block, source, query_grad, relation, out):
    return call(left_kernel, out, left_block, source.reshape(1, -1), query_grad, relation)


def coded(targets):
    meetings = targets.shape[0]
    lines = jnp.concatenate([targets // 32, targets % 32], axis=1).astype(jnp.bfloat16)
    lines = lines.reshape(meetings, -1, TE)
    lines = jnp.pad(lines, ((0, 0), (0, CODE_ROWS - lines.shape[1]), (0, 0)))
    return lines.reshape(meetings * CODE_ROWS, TE)


def shards(left_part, right_part, relation, src_index, dst_index, lengths):
    rows = left_part.shape[0]
    edges = src_index.shape[2]
    sources = src_index[0]

    held = moved(right_part, 1)
    far = moved(right_part, 7, direct)
    slots = jnp.arange(edges, dtype=jnp.int32)
    targets = jnp.where(slots[None, :] < lengths[0][:, None], dst_index[0], -1)
    codes = coded(targets)
    tables = [source_table(sources[meeting], rows) for meeting in range(4)]
    picked0 = picked_rows(left_part, tables[0])
    rows0 = moved(jnp.concatenate([picked0, codes[:CODE_ROWS]], axis=0), 6, lambda place: not direct(place))
    queries0 = queries_of(picked0, relation)
    base = picked_rows(left_part, tables[1])
    same = same_source(sources[1], sources[0])
    coeffs, query_grad, picked1 = local_meeting(0, queries0, held, codes, relation, same, base)

    rows1 = moved(picked1, 2)
    held = updated_holding(held, coeffs, queries0)
    left = updated_left(left_part, sources[0], query_grad, relation, vmem(*left_part.shape))
    relation_grad = relation_gradient(picked0, query_grad)
    middle = moved(held, 6, direct)
    grad_shape = vmem(edges, held.shape[1])
    query_grad = row_kernel(grad_kernel, grad_shape, rows1, held, relation)
    back1 = moved(query_grad, 2)
    onward = moved(rows1, 6)
    relation_grad = relation_grad + relation_gradient(rows1[:edges], query_grad)
    left = updated_left(left, sources[1], back1, relation, vmem(*left.shape))

    flag = direct(lax.axis_index("inner")).astype(jnp.int32).reshape(1)
    shape = vmem(*far.shape)
    far = row_kernel(choice_kernel, shape, rows0, far, relation, [flag], [middle])
    held = row_kernel(held_kernel, shape, onward, far, relation)
    picked2 = picked_rows(left, tables[2])
    queries2 = queries_of(picked2, relation)
    base = picked_rows(left, tables[3])
    same = same_source(sources[3], sources[2])
    coeffs, query_grad, picked3 = local_meeting(2, queries2, held, codes, relation, same, base)

    rows3 = moved(picked3, 8)
    held = updated_holding(held, coeffs, queries2)
    left = updated_left(left, sources[2], query_grad, relation, vmem(*left.shape))
    relation_grad = relation_grad + relation_gradient(picked2, query_grad)
    pieces, coeffs, query_grad, queries3 = last_meeting(rows3, held, relation, relation_grad, edges)
    sums = shared_sums(pieces)
    held = updated_holding(held, coeffs, queries3)
    held = moved(held, 8)
    last = jax.ShapeDtypeStruct(left.shape, left.dtype)
    left = updated_left(left, sources[3], moved(query_grad, 8), relation, last)
    held = call(copy_kernel, jax.ShapeDtypeStruct(held.shape, held.dtype), held)
    relation, held, left = lax.optimization_barrier((relation, held, left))
    relation_out = call(finish_kernel, jax.ShapeDtypeStruct(relation.shape, jnp.float32), sums, relation)
    return (left, held, relation_out)


def solution(mesh):
    in_specs = (
        P(AXES, None),
        P(AXES, None),
        P(),
        P(AXES, None, None),
        P(AXES, None, None),
        P(AXES, None),
    )
    out_specs = (P(AXES, None), P(AXES, None), P())
    return jax.shard_map(shards, mesh=mesh, in_specs=in_specs, out_specs=out_specs, check_vma=False)
```
